256 devices in a mesh: gx: 8 (over z), gy: 4 (over y), gz: 8 (over x, core).
Axes of the slice: x: 4, y: 4, z: 8, core: 2. Of those that a mesh axis runs over, the one named last changes fastest.
Arguments:
- points: float32 [8192, 3, 128], P(('gx', 'gy', 'gz')), may hold values from -6 to 6
- source: float32 [8192, 128], P(('gx', 'gy', 'gz')), may hold values from -6 to 6
- density: float32 [8192, 128], P(('gx', 'gy', 'gz')), may hold values from -3 to 3
- anterp: bfloat16 [8192, 216, 128], P(('gx', 'gy', 'gz')), may hold values from -0.5 to 0.5
- child_slot: int32 [8192], P(('gx', 'gy', 'gz')), may hold values from 0 to 7, as said below
- child_ops: bfloat16 [8, 216, 216], replicated, may hold values from -0.4375 to 0.4375
- parent: int32 [8192], P(('gx', 'gy', 'gz')), may hold values from 0 to 1023, as said below
- near_list: int32 [8192, 27], P(('gx', 'gy', 'gz')), may hold values from -1 to 8191, as said below
- far_list: int32 [1024, 189], P(('gx', 'gy', 'gz')), may hold values from 0 to 1023
- far_op: int32 [1024, 189], P(('gx', 'gy', 'gz')), may hold values from 0 to 15
- translations: bfloat16 [16, 216, 216], replicated, may hold values from -0.03125 to 0.03125
Outputs:
- density_out: float32 [8192, 128], P(('gx', 'gy', 'gz'))
- potential: float32 [8192, 128], P(('gx', 'gy', 'gz'))
The draws below stay inside these ranges and needn't reach their ends.
Inputs may be any that keep to these rules, and one draw needn't show every extreme that they name: Every octant has exactly 8 child leaves. Leaf l of device d = l // 32 has a parent octant owned by d or by a device next to d along gz with the same gx and gy index: parent // 4 is d - 1, d or d + 1, never past the ends of gz. `child_slot`: the 8 children of one octant have 8 different positions. `near_list`: row l lists distinct leaves: entry 0 is l itself, then other leaves b with |b - l| <= 13 on devices with the same gx and gy index as l's, then -1 in the remaining slots; at least 9 entries are listed.
All inputs are finite; a program needn't handle non-finite values.
Results may differ from the reference program's by a relative error of at most 0.008.
Values may be sent and summed in bfloat16 or wider, within the bound.
A program may use at most 64 MiB of HBM per device.

```python
import jax
import jax.numpy as jnp
from jax import lax

PTS = 128
NODES = 216
OPS = 16
INTER = 189
GHOST = 13
ITERS = 2
LEAF_DEV = 32
OCT_DEV = 4
NEAR = 27
LEAVES = 8192
OCTS = 1024
N_GZ = 8


def tree_layout(key):
    base = jax.random.fold_in(key, 11)
    key_cut, key_perm = jax.random.split(base)
    leaf_ids = jnp.arange(LEAVES, dtype=jnp.int32)
    device = leaf_ids // LEAF_DEV
    within = leaf_ids % LEAF_DEV
    column = device % N_GZ
    cuts = jax.random.randint(key_cut, (LEAVES // LEAF_DEV,), 1, 4).astype(jnp.int32)
    cut_after = jnp.take(cuts, device, axis=0)
    cut_before = jnp.take(cuts, jnp.maximum(device - 1, 0), axis=0)
    to_upper = (column < N_GZ - 1) & (within >= LEAF_DEV - cut_after)
    to_lower = (column > 0) & (within < cut_before)
    parent = jnp.where(to_upper, (device + 1) * OCT_DEV, jnp.where(to_lower, device * OCT_DEV - 1, device * OCT_DEV + within // 8))
    position = jnp.where(to_upper, within - (LEAF_DEV - cut_after), jnp.where(to_lower, 8 - cut_before + within, within % 8))
    scores = jax.random.randint(key_perm, (OCTS, 8), 0, 1 << 20) * 8 + jnp.arange(8, dtype=jnp.int32)[None, :]
    perms = jnp.argsort(scores, axis=1).astype(jnp.int32)
    slots = perms[parent, position]
    return (parent.astype(jnp.int32), slots.astype(jnp.int32))


def draw_parent(key, part):
    return tree_layout(key)[0]


def draw_child_slot(key, part):
    return tree_layout(key)[1]


def draw_near_list(key, part):
    leaf_ids = jnp.arange(LEAVES, dtype=jnp.int32)
    others = jnp.concatenate([jnp.arange(-GHOST, 0, dtype=jnp.int32), jnp.arange(1, GHOST + 1, dtype=jnp.int32)])
    key_order, key_count = jax.random.split(jax.random.fold_in(key, 23))
    ranks = jax.random.randint(key_order, (LEAVES, 2 * GHOST), 0, 1 << 20) * (2 * GHOST) + jnp.arange(2 * GHOST, dtype=jnp.int32)[None, :]
    targets = leaf_ids[:, None] + others[None, :]
    group_here = leaf_ids // LEAF_DEV // N_GZ
    same_group = (targets >= 0) & (targets < LEAVES) & (jnp.maximum(targets, 0) // LEAF_DEV // N_GZ == group_here[:, None])
    scores = jnp.where(same_group, ranks, ranks + (1 << 27))
    order = jnp.argsort(scores, axis=1)
    ordered = jnp.take_along_axis(targets, order, axis=1)
    counts = jax.random.randint(key_count, (LEAVES,), 9, NEAR + 1)
    counts = jnp.where(leaf_ids == 0, 9, counts)
    counts = jnp.minimum(counts, 1 + jnp.sum(same_group.astype(jnp.int32), axis=1))
    full_list = jnp.concatenate([leaf_ids[:, None], ordered], axis=1)
    positions = jnp.arange(NEAR, dtype=jnp.int32)
    return jnp.where(positions[None, :] < counts[:, None], full_list, -1).astype(jnp.int32)


def place_ends(values, rng, low, largest):
    longest = values.shape.index(max(values.shape))
    spots = []
    for shift in (0, 1):
        where = [jax.random.randint(jax.random.fold_in(rng, axis), (), 0, length) for axis, length in enumerate(values.shape)]
        where[longest] = (where[longest] + shift) % values.shape[longest]
        spots.append(tuple(where))
    return values.at[spots[0]].set(low).at[spots[1]].set(largest)


def shard_levels(stream_key, shape, pieces, least, top_value):
    def one(dim, parts):
        heights = jax.random.uniform(jax.random.fold_in(jax.random.fold_in(stream_key, 6), dim), (parts,), jnp.float32, least / len(pieces), top_value / len(pieces))
        return jnp.repeat(jnp.exp(heights), shape[dim] // parts).reshape((-1,) + (1,) * (len(shape) - dim - 1))

    loudness = one(*pieces[0])
    for cut in pieces[1:]:
        loudness = loudness * one(*cut)
    return loudness


def normal_values(key, extent, width, bound, cuts=(), kind=jnp.bfloat16):
    entries = width * jax.random.normal(key, extent, jnp.float32)
    if cuts:
        entries = entries * shard_levels(key, extent, cuts, -0.22, 0.18)
    return jnp.clip(entries, -bound, bound).astype(kind)


def setup_inputs(seed: int = 0) -> dict:
    arg_keys = jax.random.split(jax.random.key(seed), 12)
    return {
        "points": normal_values(arg_keys[0], (LEAVES, 3, PTS), 1.0, 6.0, ((0, 256),), jnp.float32),
        "source": normal_values(arg_keys[1], (LEAVES, PTS), 1.0, 6.0, ((0, 256),), jnp.float32),
        "density": normal_values(arg_keys[2], (LEAVES, PTS), 0.5, 3.0, ((0, 256),), jnp.float32),
        "anterp": normal_values(arg_keys[3], (LEAVES, NODES, PTS), PTS ** -0.5, 0.5, ((0, 256),)),
        "child_slot": draw_child_slot(jax.random.fold_in(arg_keys[11], 71), 0),
        "child_ops": normal_values(arg_keys[5], (8, NODES, NODES), NODES ** -0.5, 0.4375),
        "parent": draw_parent(jax.random.fold_in(arg_keys[11], 71), 0),
        "near_list": draw_near_list(jax.random.fold_in(arg_keys[11], 71), 0),
        "far_list": place_ends(jax.random.randint(arg_keys[8], (OCTS, INTER), 0, OCTS), jax.random.fold_in(arg_keys[8], 1), 0, OCTS - 1).astype(jnp.int32),
        "far_op": place_ends(jax.random.randint(arg_keys[9], (OCTS, INTER), 0, OPS), jax.random.fold_in(arg_keys[9], 1), 0, OPS - 1).astype(jnp.int32),
        "translations": normal_values(arg_keys[10], (OPS, NODES, NODES), (NODES * INTER) ** -0.5, 0.03125),
    }


SOFTEN = 0.01
DAMPING = 0.5
FAR_WEIGHT = 0.3
NEAR_WEIGHT = 0.03

def kernel_sum(target, near_points, weights):
    squared = jnp.zeros((near_points.shape[0], target.shape[1], near_points.shape[2]), jnp.float32)
    for component in range(3):
        comp_gap = target[component][None, :, None] - near_points[:, component][:, None, :]
        squared = squared + comp_gap * comp_gap
    kernel_tile = 1.0 / jnp.sqrt(squared + SOFTEN)
    return lax.optimization_barrier(jnp.sum(kernel_tile * weights[:, None, :], axis=(0, 2)))

def select_child(by_child, child_slot):
    positions = jnp.arange(8, dtype=jnp.int32)
    return lax.optimization_barrier(jnp.sum(jnp.where(child_slot[:, None, None] == positions[None, :, None], by_child, 0.0), axis=1))

def reference(points, source, density, anterp, child_slot, child_ops, parent, near_list, far_list, far_op, translations):
    highest = lax.Precision.HIGHEST
    anterp_wide = anterp.astype(jnp.float32)
    child_wide = child_ops.astype(jnp.float32)
    trans_wide = translations.astype(jnp.float32)
    op_ids = jnp.arange(OPS, dtype=jnp.int32)
    density_now = density
    potential = density
    for step in range(ITERS):

        def one_leaf(leaf_id):
            listed = near_list[leaf_id]
            is_valid = listed >= 0
            safe_ids = jnp.where(is_valid, listed, 0).astype(jnp.int32)
            near_points = jnp.take(points, safe_ids, axis=0)
            weights = jnp.where(is_valid[:, None], jnp.take(density_now, safe_ids, axis=0), 0.0)
            return kernel_sum(points[leaf_id], near_points, weights)
        near_field = lax.map(one_leaf, jnp.arange(points.shape[0], dtype=jnp.int32))
        density_b = density_now.astype(jnp.bfloat16).astype(jnp.float32)
        leaf_mult = jnp.einsum('lnp,lp->ln', anterp_wide, density_b, precision=highest).astype(jnp.bfloat16)
        by_child = jnp.einsum('cnm,lm->lcn', child_wide, leaf_mult.astype(jnp.float32), precision=highest)
        contrib = select_child(by_child, child_slot)
        multipole = jax.ops.segment_sum(contrib, parent, num_segments=OCTS).astype(jnp.bfloat16)
        multi_wide = multipole.astype(jnp.float32)

        def one_octant(octant_rows):
            listed, chosen = octant_rows
            sources = jnp.take(multi_wide, listed, axis=0)
            picked = (chosen[:, None] == op_ids[None, :]).astype(jnp.float32)
            grouped = jnp.dot(picked.T, sources, precision=highest)
            return jnp.einsum('onm,om->n', trans_wide, grouped, precision=highest)
        local_exp = lax.map(one_octant, (far_list, far_op)).astype(jnp.bfloat16)
        parent_local = jnp.take(local_exp, parent, axis=0).astype(jnp.float32)
        back_child = jnp.einsum('cnm,ln->lcm', child_wide, parent_local, precision=highest)
        leaf_local = select_child(back_child, child_slot).astype(jnp.bfloat16)
        far_field = jnp.einsum('lnp,ln->lp', anterp_wide, leaf_local.astype(jnp.float32), precision=highest)
        potential = FAR_WEIGHT * far_field + NEAR_WEIGHT * near_field
        density_now = density_now + DAMPING * (jnp.tanh(source - potential) - density_now)
    return (density_now, potential)
```

```python
import functools

import jax
import jax.numpy as jnp
from jax import lax
from jax.experimental import pallas as pl
from jax.experimental.pallas import tpu as pltpu
from jax.sharding import PartitionSpec as P

OPS = 16
ITERS = 2
SOFTEN = 0.01
DAMPING = 0.5
FAR_WEIGHT = 0.3
NEAR_WEIGHT = 0.03
PTS = 128
NODES = 216
INTER = 189
LEAF_DEV = 32
OCT_DEV = 4
NEAR = 27
HALO = 16
GHOST = 13
PAIRS = LEAF_DEV // 2
WIN = 28
SPAN = WIN * PTS
PAD = LEAF_DEV + 2 * HALO
CHUNKS = SPAN // 256

MESH = pl.DeviceIdType.MESH
F32 = jnp.float32
BF16 = jnp.bfloat16
LAST = (((1,), (1,)), ((), ()))
K_SPLIT = (0, 5, 9, 14, 16)


def iota(shape, dim):
    return lax.broadcasted_iota(jnp.int32, shape, dim)


def dot(a, b):
    return jnp.dot(a, b, preferred_element_type=F32)


def dot_last(a, b):
    return lax.dot_general(a, b, LAST, preferred_element_type=F32)


def split3(v):
    first = v.astype(BF16).astype(F32)
    rest = v - first
    second = rest.astype(BF16).astype(F32)
    third = (rest - second).astype(BF16).astype(F32)
    return first, second, third


def kernel(
    sizes,
    points, source, density, anterp, child_slot, child_ops, parent, near_list, far_list, far_op, translations,
    density_out, potential_out,
    pts_pad, q_pad, fl_prev, fl_next, fo_prev, fo_next, part_send, part_recv, table,
    src_feat, tgt_feat, feat, mask_wide, q_wide, kmat, codes, ops, counts, wide_counts, grouped, near,
    pt_ss, pt_rs, q_ss, q_rs, li_ss, li_rs, pa_ss, pa_rs, z_ss, z_rs, b_ss, b_rs, a_ss, a_rs, c_ss, c_rs,
):
    n_gx, n_gy, n_gz = sizes
    n_x = n_gz // 2
    half = n_gx * n_gy * n_x
    gx, gy, gz = lax.axis_index("gx"), lax.axis_index("gy"), lax.axis_index("gz")
    device = (gx * n_gy + gy) * n_gz + gz
    xx, core = gz // 2, gz % 2
    prev_gz, next_gz = (gz + n_gz - 1) % n_gz, (gz + 1) % n_gz
    fast = gy + core * (xx - gy)
    slow = xx + core * (gy - xx)
    n_fast = n_gy
    base = core * half

    def z_peer(s):
        return ((gx + s) % n_gx, gy, gz)

    def fast_peer(s):
        other = (fast + s) % n_fast
        return (gx, other + core * (gy - other), gz + core * (2 * other + 1 - gz))

    def slow_peer(s):
        other = (slow + s) % n_x
        return (gx, gy + core * (other - gy), 2 * other + core * (gz - 2 * other))

    sibling = (gx, gy, gz + 1 - 2 * core)
    prev_dev, next_dev = (gx, gy, prev_gz), (gx, gy, next_gz)
    outer = (gx, gy, prev_gz + core * (next_gz - prev_gz))

    barrier = pltpu.get_barrier_semaphore()
    peers = [z_peer(s) for s in range(1, n_gx)] + [fast_peer(s) for s in range(1, n_fast)]
    peers += [slow_peer(s) for s in range(1, n_x)] + [sibling, outer]
    for peer in peers:
        pl.semaphore_signal(barrier, inc=1, device_id=peer, device_id_type=MESH)

    pslot = parent[...].reshape(1, LEAF_DEV) - (device * OCT_DEV - OCT_DEV)
    cslot = child_slot[...].reshape(1, LEAF_DEV)
    square = iota((LEAF_DEV, LEAF_DEV), 0) == iota((LEAF_DEV, LEAF_DEV), 1)
    pcol = jnp.sum(jnp.where(square, pslot.astype(F32), 0.0), axis=1, keepdims=True).astype(jnp.int32)
    ccol = jnp.sum(jnp.where(square, cslot.astype(F32), 0.0), axis=1, keepdims=True).astype(jnp.int32)
    row32 = iota((32, LEAF_DEV), 0)
    part_row = 4 * (row32 // 8) + row32 % 4
    row16 = iota((16, 1), 0)

    def remote(src, dst, ss, rs, dev):
        return pltpu.make_async_remote_copy(
            src_ref=src, dst_ref=dst, send_sem=ss, recv_sem=rs, device_id=dev, device_id_type=MESH
        )

    def partial(it, q32):
        q_b = q32.astype(BF16).astype(F32)
        mult = []
        for group in range(2):
            rows = q_b[group * 16 : group * 16 + 16]
            acc = jnp.zeros((16, NODES), F32)
            for r in range(16):
                lhs = jnp.where(row16 == r, rows, 0.0).astype(BF16)
                acc = acc + dot_last(lhs, anterp[group * 16 + r])
            mult.append(acc)
        leaf_mult = jnp.concatenate(mult, axis=0).astype(BF16)
        acc = jnp.zeros((32, NODES), F32)
        for c in range(8):
            hot = jnp.where((part_row == pslot) & (cslot == c), 1.0, 0.0).astype(BF16)
            acc = acc + dot_last(dot(hot, leaf_mult).astype(BF16), child_ops[c])
        zeros = jnp.zeros((8, 256 - NODES), F32)
        for side, lo in ((0, 0), (1, 16), (2, 8)):
            part_send[it, side] = jnp.concatenate([acc[lo : lo + 8], zeros], axis=1)

    def send_partial(it):
        copies = [
            remote(part_send.at[it, 0], part_recv.at[it, 0], pa_ss.at[it, 0], pa_rs.at[it, 0], prev_dev),
            remote(part_send.at[it, 1], part_recv.at[it, 1], pa_ss.at[it, 1], pa_rs.at[it, 1], next_dev),
        ]
        for copy in copies:
            copy.start()
        return copies

    def send_q(it, src):
        copies = [
            remote(src.at[pl.ds(0, HALO)], q_pad.at[it, pl.ds(HALO + LEAF_DEV, HALO)], q_ss.at[it, 0], q_rs.at[it, 0], prev_dev),
            remote(src.at[pl.ds(HALO, HALO)], q_pad.at[it, pl.ds(0, HALO)], q_ss.at[it, 1], q_rs.at[it, 1], next_dev),
        ]
        for copy in copies:
            copy.start()
        return copies

    def own_multipole(it):
        total = part_send[it, 2] + part_recv[it, 0] + part_recv[it, 1]
        low = iota((8, PTS), 0) < 4
        mine = base + (slow * n_fast + fast) * n_gx + gx
        table[it, mine] = jnp.where(low, total[:, :128], total[:, 128:]).astype(BF16)

    def send_z(it):
        mine = base + (slow * n_fast + fast) * n_gx + gx
        block = table.at[it, pl.ds(mine, 1)]
        copies = [remote(block, block, z_ss.at[it, s - 1], z_rs.at[it, s - 1], z_peer(s)) for s in range(1, n_gx)]
        for copy in copies:
            copy.start()
        return copies

    def send_fast(it):
        block = table.at[it, pl.ds(base + (slow * n_fast + fast) * n_gx, n_gx)]
        copies = [remote(block, block, b_ss.at[it, s - 1], b_rs.at[it, s - 1], fast_peer(s)) for s in range(1, n_fast)]
        for copy in copies:
            copy.start()
        return copies

    def send_slow(it):
        block = table.at[it, pl.ds(base + slow * (n_fast * n_gx), n_fast * n_gx)]
        copies = [remote(block, block, a_ss.at[it, s - 1], a_rs.at[it, s - 1], slow_peer(s)) for s in range(1, n_x)]
        for copy in copies:
            copy.start()
        return copies

    def send_core(it):
        block = table.at[it, pl.ds(base, half)]
        copy = remote(block, block, c_ss.at[it], c_rs.at[it], sibling)
        copy.start()
        return [copy]

    def arrive(copies):
        for copy in copies:
            copy.wait_recv()

    def left(copies):
        for copy in copies:
            copy.wait_send()

    def build_source(w0, w1):
        def body(w, carry):
            y = pts_pad[w]
            y1, y2, y3 = split3(y)
            n1, n2, n3 = split3(jnp.sum(y * y, axis=0, keepdims=True))
            feat[0:3, :] = y1
            feat[3:6, :] = y1
            feat[6:9, :] = y2
            feat[9:12, :] = y2
            feat[12:15, :] = y1
            feat[15:18, :] = y3
            feat[18:19, :] = n1
            feat[19:20, :] = n2
            feat[20:21, :] = n3
            feat[21:24, :] = jnp.ones((3, PTS), F32)
            feat[24:32, :] = jnp.zeros((8, PTS), F32)
            src_feat[pl.ds(pl.multiple_of(w * PTS, PTS), PTS), :] = jnp.transpose(feat[...]).astype(BF16)
            return carry

        lax.fori_loop(w0, w1, body, 0)

    def build_target():
        def body(w, carry):
            x = points[w]
            x1, x2, x3 = split3(x)
            n1, n2, n3 = split3(jnp.sum(x * x, axis=0, keepdims=True) + SOFTEN)
            feat[0:3, :] = -2.0 * x1
            feat[3:6, :] = -2.0 * x2
            feat[6:9, :] = -2.0 * x1
            feat[9:12, :] = -2.0 * x2
            feat[12:15, :] = -2.0 * x3
            feat[15:18, :] = -2.0 * x1
            feat[18:21, :] = jnp.ones((3, PTS), F32)
            feat[21:22, :] = n1
            feat[22:23, :] = n2
            feat[23:24, :] = n3
            feat[24:32, :] = jnp.zeros((8, PTS), F32)
            tgt_feat[:, pl.ds(pl.multiple_of(w * PTS, PTS), PTS)] = feat[...].astype(BF16)
            return carry

        lax.fori_loop(0, LEAF_DEV, body, 0)

    def build_mask():
        listed = near_list[...]
        leaf = iota((LEAF_DEV, 1), 0)
        first = device * LEAF_DEV - GHOST + 2 * (leaf // 2)
        slot = jnp.where(listed >= 0, listed - first, -1)
        lane = iota((LEAF_DEV, PTS), 1)
        mask = jnp.zeros((LEAF_DEV, PTS), F32)
        for k in range(NEAR):
            mask = jnp.where(slot[:, k : k + 1] == lane, 1.0, mask)
        r = iota((8 * PAIRS, LEAF_DEV), 0)
        pick = (r // 8 * 2 + (r % 8) // 2 == iota((8 * PAIRS, LEAF_DEV), 1)) & (r % 8 < 4)
        rows = dot(jnp.where(pick, 1.0, 0.0).astype(BF16), mask.astype(BF16)).astype(BF16)
        for c in range(CHUNKS):
            spread = iota((PTS, 256), 0) == 2 * c + iota((PTS, 256), 1) // PTS
            mask_wide[:, c * 256 : c * 256 + 256] = dot(rows, jnp.where(spread, 1.0, 0.0).astype(BF16))

    def build_q(it):
        even = iota((8, PTS), 0) % 2 == 0
        for w in range(PAD):
            row = q_pad[it, w : w + 1, :]
            high = row.astype(BF16).astype(F32)
            q_wide[:, w * PTS : w * PTS + PTS] = jnp.where(even, high, row - high)

    def store_near(t, acc):
        near[pl.ds(2 * t, 1), :] = acc[0:1, :PTS] + acc[1:2, :PTS]
        near[pl.ds(2 * t + 1, 1), :] = acc[2:3, PTS:] + acc[3:4, PTS:]

    def near_lhs(t, c):
        start = pl.multiple_of((2 * t + HALO - GHOST) * PTS + c * 256, PTS)
        rows = pl.ds(pl.multiple_of(8 * t, 8), 8)
        return (mask_wide[rows, c * 256 : c * 256 + 256] * q_wide[:, pl.ds(start, 256)]).astype(BF16)

    def near_first(t0, t1):
        def body(t, carry):
            target = tgt_feat[:, pl.ds(pl.multiple_of(t * 256, 256), 256)]
            acc = jnp.zeros((8, 256), F32)
            for c in range(CHUNKS):
                start = pl.multiple_of((2 * t + HALO - GHOST) * PTS + c * 256, PTS)
                tile = lax.rsqrt(dot(src_feat[pl.ds(start, 256), :], target)).astype(BF16)
                kmat[t, c * 256 : c * 256 + 256, :] = tile
                acc = acc + dot(near_lhs(t, c), tile)
            store_near(t, acc)
            return carry

        lax.fori_loop(t0, t1, body, 0)

    def near_again(t0, t1):
        def body(t, carry):
            acc = jnp.zeros((8, 256), F32)
            for c in range(CHUNKS):
                acc = acc + dot(near_lhs(t, c), kmat[t, c * 256 : c * 256 + 256, :])
            store_near(t, acc)
            return carry

        lax.fori_loop(t0, t1, body, 0)

    def build_codes():
        lg = n_gz.bit_length() - 1
        ly = n_gy.bit_length() - 1
        for row, lists, kinds in ((0, fl_prev, fo_prev), (4, far_list, far_op), (8, fl_next, fo_next)):
            s = lists[...]
            d = s >> 2
            sz = d & (n_gz - 1)
            sy = (d >> lg) & (n_gy - 1)
            sg = d >> (lg + ly)
            sx, sc = sz >> 1, sz & 1
            spot = jnp.where(sc == 0, sx * n_gy + sy, sy * n_x + sx)
            codes[row : row + 4, :] = (sc * half + spot * n_gx + sg) * 4 + (s & 3)
            ops[row : row + 4, :] = kinds[...]

    def build_counts():
        cols = 8 * half
        width = min(256, cols)
        counts[12 * OPS :, :] = jnp.zeros((4 * OPS, cols), BF16)

        def body(g, carry):
            code = codes[pl.ds(g, 1), :]
            kind = jnp.where(iota((OPS, INTER), 0) == ops[pl.ds(g, 1), :], 1.0, 0.0).astype(BF16)
            rows = pl.ds(pl.multiple_of(g * OPS, OPS), OPS)
            for c in range(cols // width):
                hot = jnp.where(iota((width, INTER), 0) + c * width == code, 1.0, 0.0).astype(BF16)
                counts[rows, c * width : (c + 1) * width] = dot_last(kind, hot).astype(BF16)
            return carry

        lax.fori_loop(0, 12, body, 0)
        lane = iota((PTS, 256), 1)
        spread = jnp.where(iota((PTS, 256), 0) == (lane // 8) * 4 + lane % 4, 1.0, 0.0).astype(BF16)
        low = (iota((256, 256), 1) // 4) % 2 == 0
        for c in range(cols // PTS):
            both = dot(counts[:, c * PTS : (c + 1) * PTS], spread)
            wide_counts[0:256, c * 256 : (c + 1) * 256] = jnp.where(low, both, 0.0).astype(BF16)
            wide_counts[256:512, c * 256 : (c + 1) * 256] = jnp.where(low, 0.0, both).astype(BF16)

    def far_field(it):
        blocks = table[it].reshape(16 * half, PTS)
        grouped[...] = dot(wide_counts[...], blocks)
        acc = jnp.zeros((32, NODES), F32)
        for o in range(OPS):
            full = jnp.concatenate(
                [grouped[pl.ds(o, 16, stride=16), :], grouped[pl.ds(256 + o, 16, stride=16), :]], axis=1
            )[:, :NODES]
            high = full.astype(BF16)
            low = (full - high.astype(F32)).astype(BF16)
            acc = acc + dot_last(jnp.concatenate([high, low], axis=0), translations[o])
        local_exp = (acc[:16] + acc[16:]).astype(BF16)
        lane16 = iota((LEAF_DEV, 16), 1)
        acc = jnp.zeros((LEAF_DEV, NODES), F32)
        for c in range(8):
            hot = jnp.where((pcol == lane16) & (ccol == c), 1.0, 0.0).astype(BF16)
            acc = acc + dot(dot(hot, local_exp).astype(BF16), child_ops[c])
        leaf_local = acc.astype(BF16).astype(F32)
        fields = []
        for group in range(2):
            rows = leaf_local[group * 16 : group * 16 + 16]
            acc = jnp.zeros((16, PTS), F32)
            for r in range(16):
                lhs = jnp.where(row16 == r, rows, 0.0).astype(BF16)
                acc = acc + dot(lhs, anterp[group * 16 + r])
            fields.append(acc)
        return jnp.concatenate(fields, axis=0)

    own = pl.ds(HALO, LEAF_DEV)
    q_pad[0, HALO : HALO + LEAF_DEV, :] = density[...]
    partial(0, density[...])
    pl.semaphore_wait(barrier, len(peers))
    sent = send_partial(0)
    parts = sent
    halo = [
        remote(points.at[pl.ds(0, HALO)], pts_pad.at[pl.ds(HALO + LEAF_DEV, HALO)], pt_ss.at[0], pt_rs.at[0], prev_dev),
        remote(points.at[pl.ds(HALO, HALO)], pts_pad.at[pl.ds(0, HALO)], pt_ss.at[1], pt_rs.at[1], next_dev),
        remote(far_list, fl_next, li_ss.at[0], li_rs.at[0], prev_dev),
        remote(far_list, fl_prev, li_ss.at[1], li_rs.at[1], next_dev),
        remote(far_op, fo_next, li_ss.at[2], li_rs.at[2], prev_dev),
        remote(far_op, fo_prev, li_ss.at[3], li_rs.at[3], next_dev),
    ]
    for copy in halo:
        copy.start()
    halo = halo + send_q(0, density)
    sent = sent + halo
    pts_pad[own] = points[...]
    build_target()
    arrive(parts)
    own_multipole(0)
    copies = send_z(0)
    sent = sent + copies
    build_source(HALO, HALO + LEAF_DEV)
    build_mask()
    arrive(halo)
    build_source(0, HALO)
    build_source(HALO + LEAF_DEV, PAD)
    build_q(0)
    build_codes()
    near_first(K_SPLIT[0], K_SPLIT[1])
    arrive(copies)
    copies = send_fast(0)
    sent = sent + copies
    near_first(K_SPLIT[1], K_SPLIT[2])
    arrive(copies)
    copies = send_slow(0)
    sent = sent + copies
    build_counts()
    near_first(K_SPLIT[2], K_SPLIT[3])
    arrive(copies)
    copies = send_core(0)
    sent = sent + copies
    near_first(K_SPLIT[3], K_SPLIT[4])
    arrive(copies)
    potential = FAR_WEIGHT * far_field(0) + NEAR_WEIGHT * near[...]
    q = density[...]
    q = q + DAMPING * (jnp.tanh(source[...] - potential) - q)

    q_pad[1, HALO : HALO + LEAF_DEV, :] = q
    halo = send_q(1, q_pad.at[1, own])
    partial(1, q)
    parts = send_partial(1)
    sent = sent + halo + parts
    arrive(halo)
    build_q(1)
    arrive(parts)
    own_multipole(1)
    copies = send_z(1)
    sent = sent + copies
    near_again(0, PAIRS // 2)
    arrive(copies)
    copies = send_fast(1)
    sent = sent + copies
    near_again(PAIRS // 2, PAIRS)
    arrive(copies)
    copies = send_slow(1)
    sent = sent + copies
    arrive(copies)
    copies = send_core(1)
    sent = sent + copies
    arrive(copies)
    potential = FAR_WEIGHT * far_field(1) + NEAR_WEIGHT * near[...]
    q = q_pad[1, HALO : HALO + LEAF_DEV, :]
    potential_out[...] = potential
    density_out[...] = q + DAMPING * (jnp.tanh(source[...] - potential) - q)
    left(sent)


def solution(mesh):
    sizes = (mesh.shape["gx"], mesh.shape["gy"], mesh.shape["gz"])
    n_gx, n_gy, n_gz = sizes
    blocks = n_gx * n_gy * n_gz
    cols = 4 * blocks
    vmem = pl.BlockSpec(memory_space=pltpu.VMEM)
    dma = pltpu.SemaphoreType.DMA

    def shards(*args):
        return pl.pallas_call(
            functools.partial(kernel, sizes),
            out_shape=(jax.ShapeDtypeStruct((LEAF_DEV, PTS), F32),) * 2,
            in_specs=[vmem] * 11,
            out_specs=(vmem, vmem),
            scratch_shapes=[
                pltpu.VMEM((PAD, 3, PTS), F32),
                pltpu.VMEM((2, PAD, PTS), F32),
                pltpu.VMEM((OCT_DEV, INTER), jnp.int32),
                pltpu.VMEM((OCT_DEV, INTER), jnp.int32),
                pltpu.VMEM((OCT_DEV, INTER), jnp.int32),
                pltpu.VMEM((OCT_DEV, INTER), jnp.int32),
                pltpu.VMEM((2, 3, 8, 256), F32),
                pltpu.VMEM((2, 2, 8, 256), F32),
                pltpu.VMEM((2, blocks, 8, PTS), BF16),
                pltpu.VMEM((PAD * PTS, 32), BF16),
                pltpu.VMEM((32, LEAF_DEV * PTS), BF16),
                pltpu.VMEM((32, PTS), F32),
                pltpu.VMEM((8 * PAIRS, SPAN), F32),
                pltpu.VMEM((8, PAD * PTS), F32),
                pltpu.VMEM((PAIRS, SPAN, 256), BF16),
                pltpu.VMEM((16, INTER), jnp.int32),
                pltpu.VMEM((16, INTER), jnp.int32),
                pltpu.VMEM((256, cols), BF16),
                pltpu.VMEM((512, 2 * cols), BF16),
                pltpu.VMEM((512, PTS), F32),
                pltpu.VMEM((LEAF_DEV, PTS), F32),
                dma((2,)), dma((2,)), dma((2, 2)), dma((2, 2)), dma((4,)), dma((4,)), dma((2, 2)), dma((2, 2)),
                dma((2, n_gx - 1)), dma((2, n_gx - 1)), dma((2, n_gy - 1)), dma((2, n_gy - 1)),
                dma((2, n_gz // 2 - 1)), dma((2, n_gz // 2 - 1)), dma((2,)), dma((2,)),
            ],
            compiler_params=pltpu.CompilerParams(
                collective_id=0, has_side_effects=True, vmem_limit_bytes=60 * 1024 * 1024
            ),
        )(*args)

    whole = ("gx", "gy", "gz")
    in_specs = (
        P(whole, None, None),
        P(whole, None),
        P(whole, None),
        P(whole, None, None),
        P(whole),
        P(),
        P(whole),
        P(whole, None),
        P(whole, None),
        P(whole, None),
        P(),
    )
    out_specs = (P(whole, None), P(whole, None))
    return jax.shard_map(shards, mesh=mesh, in_specs=in_specs, out_specs=out_specs, check_vma=False)
```

```python
import functools

import jax
import jax.numpy as jnp
from jax import lax
from jax.experimental import pallas as pl
from jax.experimental.pallas import tpu as pltpu
from jax.sharding import PartitionSpec as P

OPS = 16
ITERS = 2
SOFTEN = 0.01
DAMPING = 0.5
FAR_WEIGHT = 0.3
NEAR_WEIGHT = 0.03
PTS = 128
NODES = 216
INTER = 189
LEAF_DEV = 32
OCT_DEV = 4
NEAR = 27
HALO = 16
GHOST = 13
PAIRS = LEAF_DEV // 2
WIN = 28
SPAN = WIN * PTS
PAD = LEAF_DEV + 2 * HALO
CHUNKS = SPAN // 256

MESH = pl.DeviceIdType.MESH
F32 = jnp.float32
BF16 = jnp.bfloat16
LAST = (((1,), (1,)), ((), ()))
K_SPLIT = (0, 5, 9, 14, 16)


def iota(shape, dim):
    return lax.broadcasted_iota(jnp.int32, shape, dim)


def dot(a, b):
    return jnp.dot(a, b, preferred_element_type=F32)


def dot_last(a, b):
    return lax.dot_general(a, b, LAST, preferred_element_type=F32)


def split3(v):
    first = v.astype(BF16).astype(F32)
    rest = v - first
    second = rest.astype(BF16).astype(F32)
    third = (rest - second).astype(BF16).astype(F32)
    return first, second, third


def kernel(
    sizes,
    points, source, density, anterp, child_slot, child_ops, parent, near_list, far_list, far_op, translations,
    result,
    pts_pad, q_pad, fl_prev, fl_next, fo_prev, fo_next, part_out, part_in, table,
    src_feat, tgt_feat, feat, mask_wide, q_wide, kmat, codes, ops, counts, grouped, near, trans,
    tr_sem, pt_ss, pt_rs, q_ss, q_rs, li_ss, li_rs, pa_ss, pa_rs, z_ss, z_rs, b_ss, b_rs, a_ss, a_rs, c_ss, c_rs,
):
    n_gx, n_gy, n_gz = sizes
    n_x = n_gz // 2
    gx, gy, gz = lax.axis_index("gx"), lax.axis_index("gy"), lax.axis_index("gz")
    device = (gx * n_gy + gy) * n_gz + gz
    xx, core = gz // 2, gz % 2
    prev_gz, next_gz = (gz + n_gz - 1) % n_gz, (gz + 1) % n_gz
    fast = gy + core * (xx - gy)
    slow = xx + core * (gy - xx)
    n_side = n_gy

    def z_peer(s):
        return ((gx + s) % n_gx, gy, gz)

    def fast_peer(s):
        other = (fast + s) % n_side
        return (gx, other + core * (gy - other), gz + core * (2 * other + 1 - gz))

    def slow_peer(s):
        other = (slow + s) % n_side
        return (gx, gy + core * (other - gy), 2 * other + core * (gz - 2 * other))

    sibling = (gx, gy, gz + 1 - 2 * core)
    prev_dev, next_dev = (gx, gy, prev_gz), (gx, gy, next_gz)
    outer = (gx, gy, prev_gz + core * (next_gz - prev_gz))
    outer_x = (xx + n_x - 1 + 2 * core) % n_x

    def spot(a, b):
        return (a + core * (b - a)) * n_side + b + core * (a - b)

    def piece(it, i, j):
        return table.at[it, core, spot((slow + i) % n_side, (fast + j) % n_side)]

    barrier = pltpu.get_barrier_semaphore()
    peers = [z_peer(s) for s in range(1, n_gx)] + [fast_peer(s) for s in range(1, n_side)]
    peers += [slow_peer(s) for s in range(1, n_side)] + [sibling, outer]
    for peer in peers:
        pl.semaphore_signal(barrier, inc=1, device_id=peer, device_id_type=MESH)

    load_trans = pltpu.make_async_copy(translations, trans, tr_sem)
    load_trans.start()
    pslot = parent[...].reshape(1, LEAF_DEV) - (device * OCT_DEV - OCT_DEV)
    cslot = child_slot[...].reshape(1, LEAF_DEV)
    square = iota((LEAF_DEV, LEAF_DEV), 0) == iota((LEAF_DEV, LEAF_DEV), 1)
    pcol = jnp.sum(jnp.where(square, pslot.astype(F32), 0.0), axis=1, keepdims=True).astype(jnp.int32)
    ccol = jnp.sum(jnp.where(square, cslot.astype(F32), 0.0), axis=1, keepdims=True).astype(jnp.int32)
    chip_slot = parent[...].reshape(1, LEAF_DEV) - (device - core) * OCT_DEV
    part_row = iota((16, LEAF_DEV), 0)
    part_row = jnp.where(part_row < 8, part_row, part_row - 16 + 16 * core)
    row16 = iota((16, 1), 0)

    def remote(src, dst, ss, rs, dev):
        return pltpu.make_async_remote_copy(
            src_ref=src, dst_ref=dst, send_sem=ss, recv_sem=rs, device_id=dev, device_id_type=MESH
        )

    def partial(it, q32):
        q_b = q32.astype(BF16).astype(F32)
        mult = []
        for group in range(2):
            rows = q_b[group * 16 : group * 16 + 16]
            acc = jnp.zeros((16, NODES), F32)
            for r in range(16):
                lhs = jnp.where(row16 == r, rows, 0.0).astype(BF16)
                acc = acc + dot_last(lhs, anterp[group * 16 + r])
            mult.append(acc)
        leaf_mult = jnp.concatenate(mult, axis=0).astype(BF16)
        acc = jnp.zeros((16, NODES), F32)
        for c in range(8):
            hot = jnp.where((part_row == chip_slot) & (cslot == c), 1.0, 0.0).astype(BF16)
            acc = acc + dot_last(dot(hot, leaf_mult).astype(BF16), child_ops[c])
        low = acc[:, :PTS]
        high = jnp.concatenate([acc[:, PTS:], jnp.zeros((16, 256 - NODES), F32)], axis=1)
        part_out[it, 0] = jnp.where(core == 0, high[:8], low[:8])
        part_out[it, 1] = low[8:]
        part_out[it, 2] = high[8:]
        part_out[it, 3] = jnp.where(core == 0, low[:8], high[:8])

    def send_partial(it):
        copies = [remote(part_out.at[it, 0], part_in.at[it, 0], pa_ss.at[it, 0], pa_rs.at[it, 0], sibling)]
        for h in range(2):
            copies.append(
                remote(
                    part_out.at[it, 1 + h], part_in.at[it, 2 - core], pa_ss.at[it, 1 + h], pa_rs.at[it, 2 - core],
                    (gx, gy, 2 * outer_x + h),
                )
            )
        for copy in copies:
            copy.start()
        return copies

    def own_multipole(it):
        for k in range(3):
            remote(part_out.at[it, k], part_in.at[it, k], pa_ss.at[it, k], pa_rs.at[it, k], sibling).wait_recv()
        total = part_out[it, 3] + part_in[it, 0] + part_in[it, 1] + part_in[it, 2]
        table[it, core, spot(slow, fast), gx] = total.astype(BF16)

    def send_q(it, src):
        copies = [
            remote(src.at[pl.ds(0, HALO)], q_pad.at[it, pl.ds(HALO + LEAF_DEV, HALO)], q_ss.at[it, 0], q_rs.at[it, 0], prev_dev),
            remote(src.at[pl.ds(HALO, HALO)], q_pad.at[it, pl.ds(0, HALO)], q_ss.at[it, 1], q_rs.at[it, 1], next_dev),
        ]
        for copy in copies:
            copy.start()
        return copies

    def send_z(it):
        block = table.at[it, core, spot(slow, fast), pl.ds(gx, 1)]
        copies = [remote(block, block, z_ss.at[it, s - 1], z_rs.at[it, s - 1], z_peer(s)) for s in range(1, n_gx)]
        for copy in copies:
            copy.start()
        return copies

    def fast_copies(it):
        block = piece(it, 0, 0)
        return [remote(block, block, b_ss.at[it, s - 1], b_rs.at[it, s - 1], fast_peer(s)) for s in range(1, n_side)]

    def slow_copies(it, j):
        block = piece(it, 0, j)
        return [
            remote(block, block, a_ss.at[it, s - 1, j], a_rs.at[it, s - 1, j], slow_peer(s)) for s in range(1, n_side)
        ]

    def core_copy(it, i, j):
        block = piece(it, i, j)
        return remote(block, block, c_ss.at[it, i, j], c_rs.at[it, i, j], sibling)

    def gather_start(it):
        fasts, slows, cores = fast_copies(it), slow_copies(it, 0), core_copy(it, 0, 0)
        copies = fasts + slows + [cores]
        for copy in copies:
            copy.start()
        return copies

    def gather_middle(it):
        fasts = fast_copies(it)
        sent = []
        for j in range(1, n_side):
            fasts[n_side - j - 1].wait_recv()
            copies = slow_copies(it, j) + [core_copy(it, 0, j)]
            for copy in copies:
                copy.start()
            sent += copies
        return sent

    def gather_end(it):
        sent = []
        for j in range(n_side):
            slows = slow_copies(it, j)
            for i in range(1, n_side):
                slows[n_side - i - 1].wait_recv()
                copy = core_copy(it, i, j)
                copy.start()
                sent.append(copy)
        return sent

    def gather_wait(it):
        for i in range(n_side):
            for j in range(n_side):
                core_copy(it, i, j).wait_recv()

    def arrive(copies):
        for copy in copies:
            copy.wait_recv()

    def left(copies):
        for copy in copies:
            copy.wait_send()

    def planes(rows, values):
        for f, value in enumerate(values):
            feat[f * PAD : f * PAD + rows, :] = value

    def build_source():
        parts = [split3(pts_pad[c]) for c in range(3)]
        norm = split3(pts_pad[0] * pts_pad[0] + pts_pad[1] * pts_pad[1] + pts_pad[2] * pts_pad[2])
        values = [parts[c][k] for k in (0, 0, 1, 1, 0, 2) for c in range(3)] + list(norm) + [jnp.ones((PAD, PTS), F32)] * 3
        planes(PAD, values)

        def body(w, carry):
            tile = jnp.transpose(feat[pl.ds(w, 32, stride=PAD), :]).astype(BF16)
            src_feat[pl.ds(pl.multiple_of(w * PTS, PTS), PTS), :] = tile
            return carry

        lax.fori_loop(2, PAD - 2, body, 0, unroll=4)

    def build_target():
        parts = [[-2.0 * v for v in split3(points[c])] for c in range(3)]
        norm = split3(points[0] * points[0] + points[1] * points[1] + points[2] * points[2] + SOFTEN)
        values = [parts[c][k] for k in (0, 1, 0, 1, 2, 0) for c in range(3)] + [jnp.ones((LEAF_DEV, PTS), F32)] * 3 + list(norm)
        planes(LEAF_DEV, values)
        feat[24 * PAD :, :] = jnp.zeros((8 * PAD, PTS), F32)

        def body(w, carry):
            tgt_feat[:, pl.ds(pl.multiple_of(w * PTS, PTS), PTS)] = feat[pl.ds(w, 32, stride=PAD), :].astype(BF16)
            return carry

        lax.fori_loop(0, LEAF_DEV, body, 0, unroll=4)

    def build_mask():
        listed = near_list[...]
        leaf = iota((LEAF_DEV, 1), 0)
        first = device * LEAF_DEV - GHOST + 2 * (leaf // 2)
        slot = jnp.where(listed >= 0, listed - first, -1)
        lane = iota((LEAF_DEV, PTS), 1)
        mask = jnp.zeros((LEAF_DEV, PTS), F32)
        for k in range(NEAR):
            mask = jnp.where(slot[:, k : k + 1] == lane, 1.0, mask)
        r = iota((8 * PAIRS, LEAF_DEV), 0)
        pick = (r // 8 * 2 + (r % 8) // 2 == iota((8 * PAIRS, LEAF_DEV), 1)) & (r % 8 < 4)
        rows = dot(jnp.where(pick, 1.0, 0.0).astype(BF16), mask.astype(BF16)).astype(BF16)
        for c in range(CHUNKS):
            spread = iota((PTS, 256), 0) == 2 * c + iota((PTS, 256), 1) // PTS
            mask_wide[:, c * 256 : c * 256 + 256] = dot(rows, jnp.where(spread, 1.0, 0.0).astype(BF16))

    def build_q(it):
        even = iota((8, PTS), 0) % 2 == 0
        for w in range(PAD):
            row = q_pad[it, w : w + 1, :]
            high = row.astype(BF16).astype(F32)
            q_wide[:, w * PTS : w * PTS + PTS] = jnp.where(even, high, row - high)

    def store_near(t, acc):
        near[pl.ds(2 * t, 1), :] = acc[0:1, :PTS] + acc[1:2, :PTS]
        near[pl.ds(2 * t + 1, 1), :] = acc[2:3, PTS:] + acc[3:4, PTS:]

    def near_lhs(t, c):
        start = pl.multiple_of((2 * t + HALO - GHOST) * PTS + c * 256, PTS)
        rows = pl.ds(pl.multiple_of(8 * t, 8), 8)
        return (mask_wide[rows, c * 256 : c * 256 + 256] * q_wide[:, pl.ds(start, 256)]).astype(BF16)

    def near_first(t0, t1):
        def body(t, carry):
            target = tgt_feat[:, pl.ds(pl.multiple_of(t * 256, 256), 256)]
            start = pl.multiple_of((2 * t + HALO - GHOST) * PTS, PTS)
            kmat[t] = lax.rsqrt(dot(src_feat[pl.ds(start, SPAN), :], target).astype(BF16))
            return carry

        lax.fori_loop(t0, t1, body, 0)
        near_again(t0, t1)

    def near_again(t0, t1):
        def body(t, carry):
            acc = jnp.zeros((8, 256), F32)
            for c in range(CHUNKS):
                acc = acc + dot(near_lhs(t, c), kmat[t, c * 256 : c * 256 + 256, :])
            store_near(t, acc)
            return carry

        lax.fori_loop(t0, t1, body, 0)

    def build_codes():
        lg = n_gz.bit_length() - 1
        ly = n_gy.bit_length() - 1
        for row, lists, kinds in ((0, fl_prev, fo_prev), (4, far_list, far_op), (8, fl_next, fo_next)):
            s = lists[...]
            d = s >> 2
            sx = (d & (n_gz - 1)) >> 1
            sy = (d >> lg) & (n_gy - 1)
            sg = d >> (lg + ly)
            codes[row : row + 4, :] = ((sx * n_gy + sy) * n_gx + sg) * 8 + (s & 7)
            ops[row : row + 4, :] = kinds[...]

    def build_counts():
        cols = 8 * n_side * n_side * n_gx
        width = min(256, cols)
        for start in (12 * OPS, 28 * OPS):
            grouped[start : start + 4 * OPS, :] = jnp.zeros((4 * OPS, PTS), F32)

        def body(g, carry):
            code = codes[pl.ds(g, 1), :]
            kind = jnp.where(iota((OPS, INTER), 0) == ops[pl.ds(g, 1), :], 1.0, 0.0).astype(BF16)
            rows = pl.ds(pl.multiple_of(g * OPS, OPS), OPS)
            for c in range(cols // width):
                hot = jnp.where(iota((width, INTER), 0) + c * width == code, 1.0, 0.0).astype(BF16)
                counts[rows, c * width : (c + 1) * width] = dot_last(kind, hot).astype(BF16)
            return carry

        lax.fori_loop(0, 12, body, 0)
    def far_field(it):
        cols = 8 * n_side * n_side * n_gx
        blocks = jnp.concatenate([table[it, 0].reshape(cols, PTS), table[it, 1].reshape(cols, PTS)], axis=1)
        both = dot(counts[...], blocks)
        grouped[0 : 12 * OPS, :] = both[:, :PTS]
        grouped[16 * OPS : 28 * OPS, :] = both[:, PTS:]
        acc = jnp.zeros((32, NODES), F32)
        for o in range(OPS):
            full = jnp.concatenate(
                [grouped[pl.ds(o, 16, stride=16), :], grouped[pl.ds(256 + o, 16, stride=16), :]], axis=1
            )[:, :NODES]
            high = full.astype(BF16)
            low = (full - high.astype(F32)).astype(BF16)
            acc = acc + dot_last(jnp.concatenate([high, low], axis=0), trans[o])
        local_exp = (acc[:16] + acc[16:]).astype(BF16)
        lane16 = iota((LEAF_DEV, 16), 1)
        acc = jnp.zeros((LEAF_DEV, NODES), F32)
        for c in range(8):
            hot = jnp.where((pcol == lane16) & (ccol == c), 1.0, 0.0).astype(BF16)
            acc = acc + dot(dot(hot, local_exp).astype(BF16), child_ops[c])
        leaf_local = acc.astype(BF16).astype(F32)
        fields = []
        for group in range(2):
            rows = leaf_local[group * 16 : group * 16 + 16]
            acc = jnp.zeros((16, PTS), F32)
            for r in range(16):
                lhs = jnp.where(row16 == r, rows, 0.0).astype(BF16)
                acc = acc + dot(lhs, anterp[group * 16 + r])
            fields.append(acc)
        return jnp.concatenate(fields, axis=0)

    own = pl.ds(HALO, LEAF_DEV)
    first, last = pl.ds(0, HALO), pl.ds(HALO, HALO)
    after = pl.ds(HALO + LEAF_DEV, HALO)
    q_pad[0, HALO : HALO + LEAF_DEV, :] = density[...]
    partial(0, density[...])
    pl.semaphore_wait(barrier, len(peers))
    sent = send_partial(0)
    halo = [
        remote(points.at[:, first], pts_pad.at[:, after], pt_ss.at[0], pt_rs.at[0], prev_dev),
        remote(points.at[:, last], pts_pad.at[:, first], pt_ss.at[1], pt_rs.at[1], next_dev),
    ]
    for copy in halo:
        copy.start()
    halo = halo + send_q(0, density)
    lists = [
        remote(far_list, fl_next, li_ss.at[0], li_rs.at[0], prev_dev),
        remote(far_list, fl_prev, li_ss.at[1], li_rs.at[1], next_dev),
        remote(far_op, fo_next, li_ss.at[2], li_rs.at[2], prev_dev),
        remote(far_op, fo_prev, li_ss.at[3], li_rs.at[3], next_dev),
    ]
    for copy in lists:
        copy.start()
    sent = sent + halo + lists
    for c in range(3):
        pts_pad[c, HALO : HALO + LEAF_DEV, :] = points[c]
    build_target()
    own_multipole(0)
    copies = send_z(0)
    sent = sent + copies
    build_mask()
    arrive(halo)
    build_source()
    build_q(0)
    near_first(K_SPLIT[0], K_SPLIT[1])
    arrive(copies)
    sent = sent + gather_start(0)
    near_first(K_SPLIT[1], K_SPLIT[2])
    sent = sent + gather_middle(0)
    arrive(lists)
    build_codes()
    build_counts()
    near_first(K_SPLIT[2], K_SPLIT[3])
    sent = sent + gather_end(0)
    near_first(K_SPLIT[3], K_SPLIT[4])
    load_trans.wait()
    gather_wait(0)
    potential = FAR_WEIGHT * far_field(0) + NEAR_WEIGHT * near[...]
    q = density[...]
    q = q + DAMPING * (jnp.tanh(source[...] - potential) - q)

    q_pad[1, HALO : HALO + LEAF_DEV, :] = q
    halo = send_q(1, q_pad.at[1, own])
    partial(1, q)
    sent = sent + halo + send_partial(1)
    arrive(halo)
    build_q(1)
    own_multipole(1)
    copies = send_z(1)
    sent = sent + copies
    near_again(0, PAIRS // 2)
    arrive(copies)
    sent = sent + gather_start(1)
    near_again(PAIRS // 2, PAIRS)
    sent = sent + gather_middle(1)
    sent = sent + gather_end(1)
    gather_wait(1)
    potential = FAR_WEIGHT * far_field(1) + NEAR_WEIGHT * near[...]
    q = q_pad[1, HALO : HALO + LEAF_DEV, :]
    result[0] = q + DAMPING * (jnp.tanh(source[...] - potential) - q)
    result[1] = potential
    left(sent)


def solution(mesh):
    sizes = (mesh.shape["gx"], mesh.shape["gy"], mesh.shape["gz"])
    n_gx, n_gy, n_gz = sizes
    n_side = n_gy
    cols = 4 * n_gx * n_gy * n_gz
    vmem = pl.BlockSpec(memory_space=pltpu.VMEM)
    dma = pltpu.SemaphoreType.DMA

    def shards(points, *args):
        out = pl.pallas_call(
            functools.partial(kernel, sizes),
            out_shape=jax.ShapeDtypeStruct((2, LEAF_DEV, PTS), F32),
            in_specs=[vmem] * 10 + [pl.BlockSpec(memory_space=pl.ANY)],
            out_specs=vmem,
            scratch_shapes=[
                pltpu.VMEM((3, PAD, PTS), F32),
                pltpu.VMEM((2, PAD, PTS), F32),
                pltpu.VMEM((OCT_DEV, INTER), jnp.int32),
                pltpu.VMEM((OCT_DEV, INTER), jnp.int32),
                pltpu.VMEM((OCT_DEV, INTER), jnp.int32),
                pltpu.VMEM((OCT_DEV, INTER), jnp.int32),
                pltpu.VMEM((2, 4, 8, PTS), F32),
                pltpu.VMEM((2, 3, 8, PTS), F32),
                pltpu.VMEM((2, 2, n_side * n_side, n_gx, 8, PTS), BF16),
                pltpu.VMEM((PAD * PTS, 32), BF16),
                pltpu.VMEM((32, LEAF_DEV * PTS), BF16),
                pltpu.VMEM((32 * PAD, PTS), F32),
                pltpu.VMEM((8 * PAIRS, SPAN), F32),
                pltpu.VMEM((8, PAD * PTS), F32),
                pltpu.VMEM((PAIRS, SPAN, 256), BF16),
                pltpu.VMEM((16, INTER), jnp.int32),
                pltpu.VMEM((16, INTER), jnp.int32),
                pltpu.VMEM((12 * OPS, cols), BF16),
                pltpu.VMEM((32 * OPS, PTS), F32),
                pltpu.VMEM((LEAF_DEV, PTS), F32),
                pltpu.VMEM((OPS, NODES, NODES), BF16),
                dma, dma((2,)), dma((2,)), dma((2, 2)), dma((2, 2)), dma((4,)), dma((4,)), dma((2, 3)), dma((2, 3)),
                dma((2, n_gx - 1)), dma((2, n_gx - 1)), dma((2, n_side - 1)), dma((2, n_side - 1)),
                dma((2, n_side - 1, n_side)), dma((2, n_side - 1, n_side)), dma((2, n_side, n_side)), dma((2, n_side, n_side)),
            ],
            compiler_params=pltpu.CompilerParams(
                collective_id=0, has_side_effects=True, vmem_limit_bytes=60 * 1024 * 1024
            ),
        )(jnp.transpose(points, (1, 0, 2)), *args)
        return out[0], out[1]

    whole = ("gx", "gy", "gz")
    in_specs = (
        P(whole, None, None),
        P(whole, None),
        P(whole, None),
        P(whole, None, None),
        P(whole),
        P(),
        P(whole),
        P(whole, None),
        P(whole, None),
        P(whole, None),
        P(),
    )
    out_specs = (P(whole, None), P(whole, None))
    return jax.shard_map(shards, mesh=mesh, in_specs=in_specs, out_specs=out_specs, check_vma=False)
```

```python
import functools

import jax
import jax.numpy as jnp
from jax import lax
from jax.experimental import pallas as pl
from jax.experimental.pallas import tpu as pltpu
from jax.sharding import PartitionSpec as P

OPS = 16
ITERS = 2
SOFTEN = 0.01
DAMPING = 0.5
FAR_WEIGHT = 0.3
NEAR_WEIGHT = 0.03
PTS = 128
NODES = 216
INTER = 189
LEAF_DEV = 32
OCT_DEV = 4
NEAR = 27
HALO = 16
PAIRS = LEAF_DEV // 2
SIDE = 7
CHUNKS = 2 * SIDE + 1
SPAN = CHUNKS * 256
UPPER = SIDE * 256 + PTS
PAD = LEAF_DEV + 2 * HALO

MESH = pl.DeviceIdType.MESH
F32 = jnp.float32
BF16 = jnp.bfloat16
LAST = (((1,), (1,)), ((), ()))
K_SPLIT = (0, 0, 8, 14, 16)


def iota(shape, dim):
    return lax.broadcasted_iota(jnp.int32, shape, dim)


def dot(a, b):
    return jnp.dot(a, b, preferred_element_type=F32)


def dot_last(a, b):
    return lax.dot_general(a, b, LAST, preferred_element_type=F32)


def split3(v):
    first = v.astype(BF16).astype(F32)
    rest = v - first
    second = rest.astype(BF16).astype(F32)
    third = (rest - second).astype(BF16).astype(F32)
    return first, second, third


def kernel(
    sizes,
    points, source, density, anterp, child_slot, child_ops, parent, near_list, far_list, far_op, translations,
    result,
    pts_pad, q_pad, fl_prev, fl_next, fo_prev, fo_next, part_out, part_in, table,
    src_feat, tgt_feat, feat, mask_wide, q_wide, kmat, codes, ops, counts, grouped, near, trans, rows_of,
    tr_sem, pt_ss, pt_rs, q_ss, q_rs, li_ss, li_rs, pa_ss, pa_rs, z_ss, z_rs, a_ss, a_rs, c_ss, c_rs,
):
    n_gx, n_gy, n_gz = sizes
    n_x = n_gz // 2
    gx, gy, gz = lax.axis_index("gx"), lax.axis_index("gy"), lax.axis_index("gz")
    device = (gx * n_gy + gy) * n_gz + gz
    xx, core = gz // 2, gz % 2
    prev_gz, next_gz = (gz + n_gz - 1) % n_gz, (gz + 1) % n_gz
    fast = gy + core * (xx - gy)
    slow = xx + core * (gy - xx)
    n_side = n_gy

    def z_peer(s):
        return ((gx + s) % n_gx, gy, gz)

    offsets = [(i, j) for i in range(n_side) for j in range(n_side) if i or j]
    offsets.sort(key=lambda o: min(o[0], n_side - o[0]) + min(o[1], n_side - o[1]))

    def side_peer(i, j):
        a, b = (slow + i) % n_side, (fast + j) % n_side
        return (gx, b + core * (a - b), 2 * (a + core * (b - a)) + core)

    sibling = (gx, gy, gz + 1 - 2 * core)
    prev_dev, next_dev = (gx, gy, prev_gz), (gx, gy, next_gz)
    outer = (gx, gy, prev_gz + core * (next_gz - prev_gz))
    outer_x = (xx + n_x - 1 + 2 * core) % n_x

    def spot(a, b):
        return (a + core * (b - a)) * n_side + b + core * (a - b)

    def piece(it, i, j):
        return table.at[it, core, spot((slow + i) % n_side, (fast + j) % n_side)]

    barrier = pltpu.get_barrier_semaphore()
    peers = [z_peer(s) for s in range(1, n_gx)] + [side_peer(i, j) for i, j in offsets] + [sibling, outer]
    for peer in peers:
        pl.semaphore_signal(barrier, inc=1, device_id=peer, device_id_type=MESH)

    load_trans = pltpu.make_async_copy(translations, trans, tr_sem)
    load_trans.start()
    pslot = parent[...].reshape(1, LEAF_DEV) - (device * OCT_DEV - OCT_DEV)
    cslot = child_slot[...].reshape(1, LEAF_DEV)
    square = iota((LEAF_DEV, LEAF_DEV), 0) == iota((LEAF_DEV, LEAF_DEV), 1)
    pcol = jnp.sum(jnp.where(square, pslot.astype(F32), 0.0), axis=1, keepdims=True).astype(jnp.int32)
    ccol = jnp.sum(jnp.where(square, cslot.astype(F32), 0.0), axis=1, keepdims=True).astype(jnp.int32)
    chip_slot = parent[...].reshape(1, LEAF_DEV) - (device - core) * OCT_DEV
    part_row = iota((16, LEAF_DEV), 0)
    part_row = jnp.where(part_row < 8, part_row, part_row - 16 + 16 * core)
    row16 = iota((16, 1), 0)

    def remote(src, dst, ss, rs, dev):
        return pltpu.make_async_remote_copy(
            src_ref=src, dst_ref=dst, send_sem=ss, recv_sem=rs, device_id=dev, device_id_type=MESH
        )

    def partial(it, q32):
        q_b = q32.astype(BF16).astype(F32)
        mult = []
        for group in range(2):
            rows = q_b[group * 16 : group * 16 + 16]
            acc = jnp.zeros((16, NODES), F32)
            for r in range(0, 16, 2):
                lhs = jnp.concatenate([jnp.where(row16 == r + k, rows, 0.0) for k in range(2)], axis=1).astype(BF16)
                both = jnp.concatenate([anterp[group * 16 + r], anterp[group * 16 + r + 1]], axis=1)
                acc = acc + dot_last(lhs, both)
            mult.append(acc)
        leaf_mult = jnp.concatenate(mult, axis=0).astype(BF16)
        acc = jnp.zeros((16, NODES), F32)
        for c in range(8):
            hot = jnp.where((part_row == chip_slot) & (cslot == c), 1.0, 0.0).astype(BF16)
            acc = acc + dot_last(dot(hot, leaf_mult).astype(BF16), child_ops[c])
        low = acc[:, :PTS]
        high = jnp.concatenate([acc[:, PTS:], jnp.zeros((16, 256 - NODES), F32)], axis=1)
        part_out[it, 0] = jnp.where(core == 0, high[:8], low[:8])
        part_out[it, 1] = low[8:]
        part_out[it, 2] = high[8:]
        part_out[it, 3] = jnp.where(core == 0, low[:8], high[:8])

    def send_partial(it):
        copies = [remote(part_out.at[it, 0], part_in.at[it, 0], pa_ss.at[it, 0], pa_rs.at[it, 0], sibling)]
        for h in range(2):
            copies.append(
                remote(
                    part_out.at[it, 1 + h], part_in.at[it, 2 - core], pa_ss.at[it, 1 + h], pa_rs.at[it, 2 - core],
                    (gx, gy, 2 * outer_x + h),
                )
            )
        for copy in copies:
            copy.start()
        return copies

    def own_multipole(it):
        for k in range(3):
            remote(part_out.at[it, k], part_in.at[it, k], pa_ss.at[it, k], pa_rs.at[it, k], sibling).wait_recv()
        total = part_out[it, 3] + part_in[it, 0] + part_in[it, 1] + part_in[it, 2]
        table[it, core, spot(slow, fast), gx] = total.astype(BF16)

    def send_q(it, src):
        copies = [
            remote(src.at[pl.ds(0, HALO)], q_pad.at[it, pl.ds(HALO + LEAF_DEV, HALO)], q_ss.at[it, 0], q_rs.at[it, 0], prev_dev),
            remote(src.at[pl.ds(HALO, HALO)], q_pad.at[it, pl.ds(0, HALO)], q_ss.at[it, 1], q_rs.at[it, 1], next_dev),
        ]
        for copy in copies:
            copy.start()
        return copies

    def send_z(it):
        block = table.at[it, core, spot(slow, fast), pl.ds(gx, 1)]
        copies = [remote(block, block, z_ss.at[it, s - 1], z_rs.at[it, s - 1], z_peer(s)) for s in range(1, n_gx)]
        for copy in copies:
            copy.start()
        return copies

    def side_copy(it, i, j):
        block = piece(it, 0, 0)
        return remote(block, block, a_ss.at[it, i, j], a_rs.at[it, i, j], side_peer(i, j))

    def core_copy(it, i, j):
        block = piece(it, i, j)
        return remote(block, block, c_ss.at[it, i, j], c_rs.at[it, i, j], sibling)

    def gather_start(it):
        copies = [side_copy(it, i, j) for i, j in offsets[::-1]] + [core_copy(it, 0, 0)]
        for copy in copies:
            copy.start()
        return copies

    def forward(it, batch):
        sent = []
        for i, j in batch:
            side_copy(it, i, j).wait_recv()
            copy = core_copy(it, (n_side - i) % n_side, (n_side - j) % n_side)
            copy.start()
            sent.append(copy)
        return sent

    def gather_middle(it):
        return forward(it, offsets[: len(offsets) // 2])

    def gather_end(it):
        return forward(it, offsets[len(offsets) // 2 :])

    def gather_wait(it):
        for i in range(n_side):
            for j in range(n_side):
                core_copy(it, i, j).wait_recv()

    def arrive(copies):
        for copy in copies:
            copy.wait_recv()

    def left(copies):
        for copy in copies:
            copy.wait_send()

    def planes(rows, values):
        for f, value in enumerate(values):
            feat[f * PAD : f * PAD + rows, :] = value

    def build_source():
        parts = [split3(pts_pad[c]) for c in range(3)]
        norm = split3(pts_pad[0] * pts_pad[0] + pts_pad[1] * pts_pad[1] + pts_pad[2] * pts_pad[2])
        values = [parts[c][k] for k in (0, 0, 1, 1, 0, 2) for c in range(3)] + list(norm) + [jnp.ones((PAD, PTS), F32)] * 3
        planes(PAD, values)

        def body(w, carry):
            tile = jnp.transpose(feat[pl.ds(w, 32, stride=PAD), :]).astype(BF16)
            src_feat[pl.ds(pl.multiple_of(w * PTS, PTS), PTS), :] = tile
            return carry

        lax.fori_loop(2, PAD - 2, body, 0, unroll=4)

    def build_target():
        parts = [[-2.0 * v for v in split3(pts_pad[c])] for c in range(3)]
        norm = split3(pts_pad[0] * pts_pad[0] + pts_pad[1] * pts_pad[1] + pts_pad[2] * pts_pad[2] + SOFTEN)
        values = [parts[c][k] for k in (0, 1, 0, 1, 2, 0) for c in range(3)] + [jnp.ones((PAD, PTS), F32)] * 3 + list(norm)
        planes(PAD, values)
        feat[24 * PAD :, :] = jnp.zeros((8 * PAD, PTS), F32)

        def body(w, carry):
            tgt_feat[:, pl.ds(pl.multiple_of(w * PTS, PTS), PTS)] = feat[pl.ds(w, 32, stride=PAD), :].astype(BF16)
            return carry

        lax.fori_loop(0, HALO + LEAF_DEV, body, 0, unroll=6)

    def build_mask():
        listed = near_list[...]
        leaf = iota((LEAF_DEV, 1), 0)
        first = device * LEAF_DEV - 2 * SIDE + 2 * (leaf // 2)
        slot = jnp.where(listed >= 0, listed - first, -1)
        lane = iota((LEAF_DEV, PTS), 1)
        mask = jnp.zeros((LEAF_DEV, PTS), F32)
        for k in range(NEAR):
            mask = jnp.where(slot[:, k : k + 1] == lane, 1.0, mask)
        r = iota((8 * PAIRS, LEAF_DEV), 0)
        pick = (r // 8 * 2 + (r % 8) // 2 == iota((8 * PAIRS, LEAF_DEV), 1)) & (r % 8 < 4)
        rows = dot(jnp.where(pick, 1.0, 0.0).astype(BF16), mask.astype(BF16)).astype(BF16)
        for c in range(CHUNKS):
            spread = iota((PTS, 256), 0) == 2 * c + iota((PTS, 256), 1) // PTS
            mask_wide[:, c * 256 : c * 256 + 256] = dot(rows, jnp.where(spread, 1.0, 0.0).astype(BF16))

    def build_q(it):
        even = iota((8, PTS), 0) % 2 == 0
        for w in range(PAD):
            row = q_pad[it, w : w + 1, :]
            high = row.astype(BF16).astype(F32)
            q_wide[:, w * PTS : w * PTS + PTS] = jnp.where(even, high, row - high)

    def store_near(t, acc):
        near[pl.ds(2 * t, 1), :] = acc[0:1, :PTS] + acc[1:2, :PTS]
        near[pl.ds(2 * t + 1, 1), :] = acc[2:3, PTS:] + acc[3:4, PTS:]

    def near_lhs(t, c):
        start = pl.multiple_of((t + HALO // 2 - SIDE + c) * 256, 256)
        rows = pl.ds(pl.multiple_of(8 * t, 8), 8)
        return (mask_wide[rows, c * 256 : c * 256 + 256] * q_wide[:, pl.ds(start, 256)]).astype(BF16)

    def build_halo():
        for e in range(SIDE):
            target = tgt_feat[:, (e + 1) * 256 : (e + 2) * 256]
            tile = dot(src_feat[HALO * PTS : HALO * PTS + (e + 1) * 256 - PTS, :], target)
            kmat[e, (SIDE - e) * 256 :, :] = lax.rsqrt(tile.astype(BF16))

    def near_again(t0, t1):
        def body(t, carry):
            acc = jnp.zeros((8, 256), F32)
            for o in range(SIDE):
                acc = acc + dot(near_lhs(t, SIDE + o), kmat[t + SIDE, o * 256 : o * 256 + 256, :])
            acc = acc + dot(near_lhs(t, 2 * SIDE)[:, :PTS], kmat[t + SIDE, SIDE * 256 :, :])
            for o in range(1, SIDE):
                acc = acc + dot_last(near_lhs(t, SIDE - o), kmat[t + SIDE - o, o * 256 : o * 256 + 256, :])
            edge = dot_last(near_lhs(t, 0), kmat[t, SIDE * 256 :, :])
            acc = acc + jnp.concatenate([edge, jnp.zeros((8, PTS), F32)], axis=1)
            store_near(t, acc)
            return carry

        lax.fori_loop(t0, t1, body, 0, unroll=2)

    def near_first(t0, t1):
        def body(t, carry):
            start = pl.multiple_of((t + HALO // 2) * 256, 256)
            target = tgt_feat[:, pl.ds(start, 256)]
            kmat[t + SIDE] = lax.rsqrt(dot(src_feat[pl.ds(start, UPPER), :], target).astype(BF16))
            return carry

        lax.fori_loop(t0, t1, body, 0, unroll=2)
        near_again(t0, t1)

    def build_codes():
        lg = n_gz.bit_length() - 1
        ly = n_gy.bit_length() - 1
        for row, lists, kinds in ((0, fl_prev, fo_prev), (4, far_list, far_op), (8, fl_next, fo_next)):
            s = lists[...]
            d = s >> 2
            sx = (d & (n_gz - 1)) >> 1
            sy = (d >> lg) & (n_gy - 1)
            sg = d >> (lg + ly)
            codes[row : row + 4, :] = ((sx * n_gy + sy) * n_gx + sg) * 8 + (s & 7)
            ops[row : row + 4, :] = kinds[...]

    def build_counts():
        cols = 8 * n_side * n_side * n_gx
        width = min(256, cols)
        rows_of[...] = iota((cols, INTER), 0).astype(jnp.int16)
        for start in (12 * OPS, 28 * OPS):
            grouped[start : start + 4 * OPS, :] = jnp.zeros((4 * OPS, PTS), F32)

        def body(g, carry):
            code16 = jnp.broadcast_to(codes[pl.ds(g, 1), :], (16, INTER)).astype(jnp.int16)
            code16 = jnp.broadcast_to(code16[:1], (width, INTER))
            one16, zero16 = jnp.ones((width, INTER), BF16), jnp.zeros((width, INTER), BF16)
            kind = jnp.where(iota((OPS, INTER), 0) == ops[pl.ds(g, 1), :], 1.0, 0.0).astype(BF16)
            rows = pl.ds(pl.multiple_of(g * OPS, OPS), OPS)
            for c in range(cols // width):
                hot = jnp.where(rows_of[c * width : (c + 1) * width, :] == code16, one16, zero16)
                counts[rows, c * width : (c + 1) * width] = dot_last(kind, hot).astype(BF16)
            return carry

        lax.fori_loop(0, 12, body, 0)
    def far_field(it):
        gather_wait(it)
        cols = 8 * n_side * n_side * n_gx
        blocks = jnp.concatenate([table[it, 0].reshape(cols, PTS), table[it, 1].reshape(cols, PTS)], axis=1)
        both = dot(counts[...], blocks)
        grouped[0 : 12 * OPS, :] = both[:, :PTS]
        grouped[16 * OPS : 28 * OPS, :] = both[:, PTS:]
        acc = jnp.zeros((32, NODES), F32)
        for o in range(OPS):
            full = jnp.concatenate(
                [grouped[pl.ds(o, 16, stride=16), :], grouped[pl.ds(256 + o, 16, stride=16), :]], axis=1
            )[:, :NODES]
            high = full.astype(BF16)
            low = (full - high.astype(F32)).astype(BF16)
            acc = acc + dot_last(jnp.concatenate([high, low], axis=0), trans[o])
        local_exp = (acc[:16] + acc[16:]).astype(BF16)
        lane16 = iota((LEAF_DEV, 16), 1)
        acc = jnp.zeros((LEAF_DEV, NODES), F32)
        for c in range(8):
            hot = jnp.where((pcol == lane16) & (ccol == c), 1.0, 0.0).astype(BF16)
            acc = acc + dot(dot(hot, local_exp).astype(BF16), child_ops[c])
        leaf_local = acc.astype(BF16)
        fields = []
        for group in range(2):
            rows = leaf_local[group * 16 : group * 16 + 16]
            acc = jnp.zeros((16, PTS), F32)
            for r in range(0, 16, 2):
                both = jnp.concatenate([anterp[group * 16 + r], anterp[group * 16 + r + 1]], axis=1)
                pair = dot(rows, both)
                acc = jnp.where(row16 == r, pair[:, :PTS], jnp.where(row16 == r + 1, pair[:, PTS:], acc))
            fields.append(acc)
        return jnp.concatenate(fields, axis=0)

    own = pl.ds(HALO, LEAF_DEV)
    first, last = pl.ds(0, HALO), pl.ds(HALO, HALO)
    after = pl.ds(HALO + LEAF_DEV, HALO)
    q_pad[0, HALO : HALO + LEAF_DEV, :] = density[...]
    partial(0, density[...])
    pl.semaphore_wait(barrier, len(peers))
    sent = send_partial(0)
    halo = [
        remote(points.at[:, first], pts_pad.at[:, after], pt_ss.at[0], pt_rs.at[0], prev_dev),
        remote(points.at[:, last], pts_pad.at[:, first], pt_ss.at[1], pt_rs.at[1], next_dev),
    ]
    for copy in halo:
        copy.start()
    halo = halo + send_q(0, density)
    lists = [
        remote(far_list, fl_next, li_ss.at[0], li_rs.at[0], prev_dev),
        remote(far_list, fl_prev, li_ss.at[1], li_rs.at[1], next_dev),
        remote(far_op, fo_next, li_ss.at[2], li_rs.at[2], prev_dev),
        remote(far_op, fo_prev, li_ss.at[3], li_rs.at[3], next_dev),
    ]
    for copy in lists:
        copy.start()
    sent = sent + halo + lists
    for c in range(3):
        pts_pad[c, HALO : HALO + LEAF_DEV, :] = points[c]
    build_mask()
    own_multipole(0)
    copies = send_z(0)
    sent = sent + copies
    arrive(halo)
    build_target()
    build_source()
    build_halo()
    build_q(0)
    near_first(K_SPLIT[0], K_SPLIT[1])
    arrive(copies)
    sent = sent + gather_start(0)
    near_first(K_SPLIT[1], K_SPLIT[2])
    sent = sent + gather_middle(0)
    arrive(lists)
    build_codes()
    build_counts()
    near_first(K_SPLIT[2], K_SPLIT[3])
    sent = sent + gather_end(0)
    near_first(K_SPLIT[3], K_SPLIT[4])
    load_trans.wait()
    potential = FAR_WEIGHT * far_field(0) + NEAR_WEIGHT * near[...]
    q = density[...]
    q = q + DAMPING * (jnp.tanh(source[...] - potential) - q)

    q_pad[1, HALO : HALO + LEAF_DEV, :] = q
    halo = send_q(1, q_pad.at[1, own])
    partial(1, q)
    sent = sent + halo + send_partial(1)
    arrive(halo)
    build_q(1)
    own_multipole(1)
    copies = send_z(1)
    sent = sent + copies
    near_again(0, PAIRS // 2)
    arrive(copies)
    sent = sent + gather_start(1)
    near_again(PAIRS // 2, PAIRS)
    sent = sent + gather_middle(1)
    sent = sent + gather_end(1)
    potential = FAR_WEIGHT * far_field(1) + NEAR_WEIGHT * near[...]
    q = q_pad[1, HALO : HALO + LEAF_DEV, :]
    result[0] = q + DAMPING * (jnp.tanh(source[...] - potential) - q)
    result[1] = potential
    left(sent)


def solution(mesh):
    sizes = (mesh.shape["gx"], mesh.shape["gy"], mesh.shape["gz"])
    n_gx, n_gy, n_gz = sizes
    n_side = n_gy
    cols = 4 * n_gx * n_gy * n_gz
    vmem = pl.BlockSpec(memory_space=pltpu.VMEM)
    dma = pltpu.SemaphoreType.DMA

    def shards(points, *args):
        out = pl.pallas_call(
            functools.partial(kernel, sizes),
            out_shape=jax.ShapeDtypeStruct((2, LEAF_DEV, PTS), F32),
            in_specs=[vmem] * 10 + [pl.BlockSpec(memory_space=pl.ANY)],
            out_specs=vmem,
            scratch_shapes=[
                pltpu.VMEM((3, PAD, PTS), F32),
                pltpu.VMEM((2, PAD, PTS), F32),
                pltpu.VMEM((OCT_DEV, INTER), jnp.int32),
                pltpu.VMEM((OCT_DEV, INTER), jnp.int32),
                pltpu.VMEM((OCT_DEV, INTER), jnp.int32),
                pltpu.VMEM((OCT_DEV, INTER), jnp.int32),
                pltpu.VMEM((2, 4, 8, PTS), F32),
                pltpu.VMEM((2, 3, 8, PTS), F32),
                pltpu.VMEM((2, 2, n_side * n_side, n_gx, 8, PTS), BF16),
                pltpu.VMEM((PAD * PTS, 32), BF16),
                pltpu.VMEM((32, (HALO + LEAF_DEV) * PTS), BF16),
                pltpu.VMEM((32 * PAD, PTS), F32),
                pltpu.VMEM((8 * PAIRS, SPAN), F32),
                pltpu.VMEM((8, PAD * PTS), F32),
                pltpu.VMEM((PAIRS + SIDE, UPPER, 256), BF16),
                pltpu.VMEM((16, INTER), jnp.int32),
                pltpu.VMEM((16, INTER), jnp.int32),
                pltpu.VMEM((12 * OPS, cols), BF16),
                pltpu.VMEM((32 * OPS, PTS), F32),
                pltpu.VMEM((LEAF_DEV, PTS), F32),
                pltpu.VMEM((OPS, NODES, NODES), BF16),
                pltpu.VMEM((cols, INTER), jnp.int16),
                dma, dma((2,)), dma((2,)), dma((2, 2)), dma((2, 2)), dma((4,)), dma((4,)), dma((2, 3)), dma((2, 3)),
                dma((2, n_gx - 1)), dma((2, n_gx - 1)),
                dma((2, n_side, n_side)), dma((2, n_side, n_side)), dma((2, n_side, n_side)), dma((2, n_side, n_side)),
            ],
            compiler_params=pltpu.CompilerParams(
                collective_id=0, has_side_effects=True, vmem_limit_bytes=60 * 1024 * 1024
            ),
        )(jnp.transpose(points, (1, 0, 2)), *args)
        return out[0], out[1]

    whole = ("gx", "gy", "gz")
    in_specs = (
        P(whole, None, None),
        P(whole, None),
        P(whole, None),
        P(whole, None, None),
        P(whole),
        P(),
        P(whole),
        P(whole, None),
        P(whole, None),
        P(whole, None),
        P(),
    )
    out_specs = (P(whole, None), P(whole, None))
    return jax.shard_map(shards, mesh=mesh, in_specs=in_specs, out_specs=out_specs, check_vma=False)
```

```python
import functools

import jax
import jax.numpy as jnp
from jax import lax
from jax.experimental import pallas as pl
from jax.experimental.pallas import tpu as pltpu
from jax.sharding import PartitionSpec as P

OPS = 16
ITERS = 2
SOFTEN = 0.01
DAMPING = 0.5
FAR_WEIGHT = 0.3
NEAR_WEIGHT = 0.03
PTS = 128
NODES = 216
INTER = 189
LEAF_DEV = 32
OCT_DEV = 4
NEAR = 27
HALO = 16
PAIRS = LEAF_DEV // 2
SIDE = 7
CHUNKS = 2 * SIDE + 1
SPAN = CHUNKS * 256
UPPER = SIDE * 256 + PTS
PAD = LEAF_DEV + 2 * HALO

MESH = pl.DeviceIdType.MESH
F32 = jnp.float32
BF16 = jnp.bfloat16
LAST = (((1,), (1,)), ((), ()))
K_SPLIT = (0, 0, 8, 14, 16)


def iota(shape, dim):
    return lax.broadcasted_iota(jnp.int32, shape, dim)


def dot(a, b):
    return jnp.dot(a, b, preferred_element_type=F32)


def dot_last(a, b):
    return lax.dot_general(a, b, LAST, preferred_element_type=F32)


def split3(v):
    first = v.astype(BF16).astype(F32)
    rest = v - first
    second = rest.astype(BF16).astype(F32)
    third = (rest - second).astype(BF16).astype(F32)
    return first, second, third


def kernel(
    sizes,
    points_hbm, source_hbm, density_hbm, anterp_hbm, child_slot_hbm, child_ops_hbm, parent_hbm, near_list_hbm, far_list_hbm, far_op_hbm, translations_hbm,
    result,
    pts_pad, q_pad, fl_prev, fl_next, fo_prev, fo_next, part_out, part_in, table,
    src_feat, tgt_feat, feat, mask_wide, q_wide, kmat, codes, ops, counts, grouped, near, trans, rows_of,
    points, source, density, anterp, child_slot, child_ops, parent, near_list, far_list, far_op,
    load_sem, tr_sem, pt_ss, pt_rs, q_ss, q_rs, li_ss, li_rs, pa_ss, pa_rs, z_ss, z_rs, a_ss, a_rs, c_ss, c_rs,
):
    n_gx, n_gy, n_gz = sizes
    n_x = n_gz // 2
    gx, gy, gz = lax.axis_index("gx"), lax.axis_index("gy"), lax.axis_index("gz")
    device = (gx * n_gy + gy) * n_gz + gz
    xx, core = gz // 2, gz % 2
    prev_gz, next_gz = (gz + n_gz - 1) % n_gz, (gz + 1) % n_gz
    fast = gy + core * (xx - gy)
    slow = xx + core * (gy - xx)
    n_side = n_gy

    def z_peer(s):
        return ((gx + s) % n_gx, gy, gz)

    offsets = [(i, j) for i in range(n_side) for j in range(n_side) if i or j]
    offsets.sort(key=lambda o: min(o[0], n_side - o[0]) + min(o[1], n_side - o[1]))

    def side_peer(i, j):
        a, b = (slow + i) % n_side, (fast + j) % n_side
        return (gx, b + core * (a - b), 2 * (a + core * (b - a)) + core)

    sibling = (gx, gy, gz + 1 - 2 * core)
    prev_dev, next_dev = (gx, gy, prev_gz), (gx, gy, next_gz)
    outer = (gx, gy, prev_gz + core * (next_gz - prev_gz))
    outer_x = (xx + n_x - 1 + 2 * core) % n_x

    def spot(a, b):
        return (a + core * (b - a)) * n_side + b + core * (a - b)

    def piece(it, i, j):
        return table.at[it, core, spot((slow + i) % n_side, (fast + j) % n_side)]

    barrier = pltpu.get_barrier_semaphore()
    peers = [z_peer(s) for s in range(1, n_gx)] + [side_peer(i, j) for i, j in offsets] + [sibling, outer]
    for peer in peers:
        pl.semaphore_signal(barrier, inc=1, device_id=peer, device_id_type=MESH)

    loads = [
        pltpu.make_async_copy(src, dst, load_sem.at[k])
        for k, (src, dst) in enumerate(
            (
                (density_hbm, density), (parent_hbm, parent), (child_slot_hbm, child_slot), (near_list_hbm, near_list),
                (points_hbm, points), (far_list_hbm, far_list), (far_op_hbm, far_op), (source_hbm, source),
                (anterp_hbm, anterp), (child_ops_hbm, child_ops),
            )
        )
    ]
    for load in loads:
        load.start()
    load_trans = pltpu.make_async_copy(translations_hbm, trans, tr_sem)
    load_trans.start()
    for load in loads[:3]:
        load.wait()
    pslot = parent[...].reshape(1, LEAF_DEV) - (device * OCT_DEV - OCT_DEV)
    cslot = child_slot[...].reshape(1, LEAF_DEV)
    square = iota((LEAF_DEV, LEAF_DEV), 0) == iota((LEAF_DEV, LEAF_DEV), 1)
    pcol = jnp.sum(jnp.where(square, pslot.astype(F32), 0.0), axis=1, keepdims=True).astype(jnp.int32)
    ccol = jnp.sum(jnp.where(square, cslot.astype(F32), 0.0), axis=1, keepdims=True).astype(jnp.int32)
    chip_slot = parent[...].reshape(1, LEAF_DEV) - (device - core) * OCT_DEV
    part_row = iota((16, LEAF_DEV), 0)
    part_row = jnp.where(part_row < 8, part_row, part_row - 16 + 16 * core)
    row16 = iota((16, 1), 0)

    def remote(src, dst, ss, rs, dev):
        return pltpu.make_async_remote_copy(
            src_ref=src, dst_ref=dst, send_sem=ss, recv_sem=rs, device_id=dev, device_id_type=MESH
        )

    def partial(it, q32):
        q_b = q32.astype(BF16).astype(F32)
        mult = []
        for group in range(2):
            rows = q_b[group * 16 : group * 16 + 16]
            acc = jnp.zeros((16, NODES), F32)
            for r in range(0, 16, 2):
                lhs = jnp.concatenate([jnp.where(row16 == r + k, rows, 0.0) for k in range(2)], axis=1).astype(BF16)
                both = jnp.concatenate([anterp[group * 16 + r], anterp[group * 16 + r + 1]], axis=1)
                acc = acc + dot_last(lhs, both)
            mult.append(acc)
        leaf_mult = jnp.concatenate(mult, axis=0).astype(BF16)
        acc = jnp.zeros((16, NODES), F32)
        for c in range(8):
            hot = jnp.where((part_row == chip_slot) & (cslot == c), 1.0, 0.0).astype(BF16)
            acc = acc + dot_last(dot(hot, leaf_mult).astype(BF16), child_ops[c])
        low = acc[:, :PTS]
        high = jnp.concatenate([acc[:, PTS:], jnp.zeros((16, 256 - NODES), F32)], axis=1)
        part_out[it, 0] = jnp.where(core == 0, high[:8], low[:8])
        part_out[it, 1] = low[8:]
        part_out[it, 2] = high[8:]
        part_out[it, 3] = jnp.where(core == 0, low[:8], high[:8])

    def send_partial(it):
        copies = [remote(part_out.at[it, 0], part_in.at[it, 0], pa_ss.at[it, 0], pa_rs.at[it, 0], sibling)]
        for h in range(2):
            copies.append(
                remote(
                    part_out.at[it, 1 + h], part_in.at[it, 2 - core], pa_ss.at[it, 1 + h], pa_rs.at[it, 2 - core],
                    (gx, gy, 2 * outer_x + h),
                )
            )
        for copy in copies:
            copy.start()
        return copies

    def own_multipole(it):
        for k in range(3):
            remote(part_out.at[it, k], part_in.at[it, k], pa_ss.at[it, k], pa_rs.at[it, k], sibling).wait_recv()
        total = part_out[it, 3] + part_in[it, 0] + part_in[it, 1] + part_in[it, 2]
        table[it, core, spot(slow, fast), gx] = total.astype(BF16)

    def send_q(it, src):
        copies = [
            remote(src.at[pl.ds(0, HALO)], q_pad.at[it, pl.ds(HALO + LEAF_DEV, HALO)], q_ss.at[it, 0], q_rs.at[it, 0], prev_dev),
            remote(src.at[pl.ds(HALO, HALO)], q_pad.at[it, pl.ds(0, HALO)], q_ss.at[it, 1], q_rs.at[it, 1], next_dev),
        ]
        for copy in copies:
            copy.start()
        return copies

    def send_z(it):
        block = table.at[it, core, spot(slow, fast), pl.ds(gx, 1)]
        copies = [remote(block, block, z_ss.at[it, s - 1], z_rs.at[it, s - 1], z_peer(s)) for s in range(1, n_gx)]
        for copy in copies:
            copy.start()
        return copies

    def side_copy(it, i, j):
        block = piece(it, 0, 0)
        return remote(block, block, a_ss.at[it, i, j], a_rs.at[it, i, j], side_peer(i, j))

    def core_copy(it, i, j):
        block = piece(it, i, j)
        return remote(block, block, c_ss.at[it, i, j], c_rs.at[it, i, j], sibling)

    def gather_start(it):
        copies = [side_copy(it, i, j) for i, j in offsets[::-1]] + [core_copy(it, 0, 0)]
        for copy in copies:
            copy.start()
        return copies

    def forward(it, batch):
        sent = []
        for i, j in batch:
            side_copy(it, i, j).wait_recv()
            copy = core_copy(it, (n_side - i) % n_side, (n_side - j) % n_side)
            copy.start()
            sent.append(copy)
        return sent

    def gather_middle(it):
        return forward(it, offsets[: len(offsets) // 2])

    def gather_end(it):
        return forward(it, offsets[len(offsets) // 2 :])

    def gather_wait(it):
        for i in range(n_side):
            for j in range(n_side):
                core_copy(it, i, j).wait_recv()

    def arrive(copies):
        for copy in copies:
            copy.wait_recv()

    def left(copies):
        for copy in copies:
            copy.wait_send()

    def planes(lo, hi, values):
        for f, value in enumerate(values):
            feat[f * PAD + lo : f * PAD + hi, :] = value

    def build_source():
        parts = [split3(pts_pad[c]) for c in range(3)]
        norm = split3(pts_pad[0] * pts_pad[0] + pts_pad[1] * pts_pad[1] + pts_pad[2] * pts_pad[2])
        values = [parts[c][k] for k in (0, 0, 1, 1, 0, 2) for c in range(3)] + list(norm) + [jnp.ones((PAD, PTS), F32)] * 3
        planes(0, PAD, values)

        def body(w, carry):
            tile = jnp.transpose(feat[pl.ds(w, 32, stride=PAD), :]).astype(BF16)
            src_feat[pl.ds(pl.multiple_of(w * PTS, PTS), PTS), :] = tile
            return carry

        lax.fori_loop(2, PAD - 2, body, 0, unroll=4)

    def build_target(lo, hi):
        pts = [pts_pad[c, lo:hi] for c in range(3)]
        parts = [[-2.0 * v for v in split3(p)] for p in pts]
        norm = split3(pts[0] * pts[0] + pts[1] * pts[1] + pts[2] * pts[2] + SOFTEN)
        values = [parts[c][k] for k in (0, 1, 0, 1, 2, 0) for c in range(3)]
        planes(lo, hi, values + [jnp.ones((hi - lo, PTS), F32)] * 3 + list(norm))

        def body(w, carry):
            tgt_feat[:, pl.ds(pl.multiple_of(w * PTS, PTS), PTS)] = feat[pl.ds(w, 32, stride=PAD), :].astype(BF16)
            return carry

        lax.fori_loop(lo, hi, body, 0, unroll=8)

    def build_mask():
        listed = near_list[...]
        leaf = iota((LEAF_DEV, 1), 0)
        first = device * LEAF_DEV - 2 * SIDE + 2 * (leaf // 2)
        slot = jnp.where(listed >= 0, listed - first, -1)
        lane = iota((LEAF_DEV, PTS), 1)
        mask = jnp.zeros((LEAF_DEV, PTS), F32)
        for k in range(NEAR):
            mask = jnp.where(slot[:, k : k + 1] == lane, 1.0, mask)
        r = iota((8 * PAIRS, LEAF_DEV), 0)
        pick = (r // 8 * 2 + (r % 8) // 2 == iota((8 * PAIRS, LEAF_DEV), 1)) & (r % 8 < 4)
        rows = dot(jnp.where(pick, 1.0, 0.0).astype(BF16), mask.astype(BF16)).astype(BF16)
        for c in range(CHUNKS):
            spread = iota((PTS, 256), 0) == 2 * c + iota((PTS, 256), 1) // PTS
            mask_wide[:, c * 256 : c * 256 + 256] = dot(rows, jnp.where(spread, 1.0, 0.0).astype(BF16))

    def build_q(it):
        even = iota((8, PTS), 0) % 2 == 0
        for w in range(PAD):
            row = q_pad[it, w : w + 1, :]
            high = row.astype(BF16).astype(F32)
            q_wide[:, w * PTS : w * PTS + PTS] = jnp.where(even, high, row - high)

    def store_near(t, acc):
        near[pl.ds(2 * t, 1), :] = acc[0:1, :PTS] + acc[1:2, :PTS]
        near[pl.ds(2 * t + 1, 1), :] = acc[2:3, PTS:] + acc[3:4, PTS:]

    def near_lhs(t, c):
        start = pl.multiple_of((t + HALO // 2 - SIDE + c) * 256, 256)
        rows = pl.ds(pl.multiple_of(8 * t, 8), 8)
        return (mask_wide[rows, c * 256 : c * 256 + 256] * q_wide[:, pl.ds(start, 256)]).astype(BF16)

    def build_halo():
        for e in range(SIDE):
            target = tgt_feat[:, (e + 1) * 256 : (e + 2) * 256]
            tile = dot(src_feat[HALO * PTS : HALO * PTS + (e + 1) * 256 - PTS, :], target)
            kmat[e, (SIDE - e) * 256 :, :] = lax.rsqrt(tile.astype(BF16))

    def near_again(t0, t1):
        def body(t, carry):
            acc = jnp.zeros((8, 256), F32)
            for o in range(SIDE):
                acc = acc + dot(near_lhs(t, SIDE + o), kmat[t + SIDE, o * 256 : o * 256 + 256, :])
            acc = acc + dot(near_lhs(t, 2 * SIDE)[:, :PTS], kmat[t + SIDE, SIDE * 256 :, :])
            for o in range(1, SIDE):
                acc = acc + dot_last(near_lhs(t, SIDE - o), kmat[t + SIDE - o, o * 256 : o * 256 + 256, :])
            edge = dot_last(near_lhs(t, 0), kmat[t, SIDE * 256 :, :])
            acc = acc + jnp.concatenate([edge, jnp.zeros((8, PTS), F32)], axis=1)
            store_near(t, acc)
            return carry

        lax.fori_loop(t0, t1, body, 0, unroll=2)

    def near_first(t0, t1):
        def body(t, carry):
            start = pl.multiple_of((t + HALO // 2) * 256, 256)
            target = tgt_feat[:, pl.ds(start, 256)]
            kmat[t + SIDE] = lax.rsqrt(dot(src_feat[pl.ds(start, UPPER), :], target).astype(BF16))
            return carry

        lax.fori_loop(t0, t1, body, 0, unroll=2)
        near_again(t0, t1)

    def build_codes():
        lg = n_gz.bit_length() - 1
        ly = n_gy.bit_length() - 1
        for row, lists, kinds in ((0, fl_prev, fo_prev), (4, far_list, far_op), (8, fl_next, fo_next)):
            s = lists[...]
            d = s >> 2
            sx = (d & (n_gz - 1)) >> 1
            sy = (d >> lg) & (n_gy - 1)
            sg = d >> (lg + ly)
            codes[row : row + 4, :] = ((sx * n_gy + sy) * n_gx + sg) * 8 + (s & 7)
            ops[row : row + 4, :] = kinds[...]

    def build_counts():
        cols = 8 * n_side * n_side * n_gx
        width = min(256, cols)
        rows_of[...] = iota((cols, INTER), 0).astype(jnp.int16)
        for start in (12 * OPS, 28 * OPS):
            grouped[start : start + 4 * OPS, :] = jnp.zeros((4 * OPS, PTS), F32)

        def body(g, carry):
            code16 = jnp.broadcast_to(codes[pl.ds(g, 1), :], (16, INTER)).astype(jnp.int16)
            code16 = jnp.broadcast_to(code16[:1], (width, INTER))
            one16, zero16 = jnp.ones((width, INTER), BF16), jnp.zeros((width, INTER), BF16)
            kind = jnp.where(iota((OPS, INTER), 0) == ops[pl.ds(g, 1), :], 1.0, 0.0).astype(BF16)
            rows = pl.ds(pl.multiple_of(g * OPS, OPS), OPS)
            for c in range(cols // width):
                hot = jnp.where(rows_of[c * width : (c + 1) * width, :] == code16, one16, zero16)
                counts[rows, c * width : (c + 1) * width] = dot_last(kind, hot).astype(BF16)
            return carry

        lax.fori_loop(0, 12, body, 0)
    def far_field(it):
        gather_wait(it)
        cols = 8 * n_side * n_side * n_gx
        blocks = jnp.concatenate([table[it, 0].reshape(cols, PTS), table[it, 1].reshape(cols, PTS)], axis=1)
        both = dot(counts[...], blocks)
        grouped[0 : 12 * OPS, :] = both[:, :PTS]
        grouped[16 * OPS : 28 * OPS, :] = both[:, PTS:]
        acc = jnp.zeros((32, NODES), F32)
        for o in range(OPS):
            full = jnp.concatenate(
                [grouped[pl.ds(o, 16, stride=16), :], grouped[pl.ds(256 + o, 16, stride=16), :]], axis=1
            )[:, :NODES]
            high = full.astype(BF16)
            low = (full - high.astype(F32)).astype(BF16)
            acc = acc + dot_last(jnp.concatenate([high, low], axis=0), trans[o])
        local_exp = (acc[:16] + acc[16:]).astype(BF16)
        lane16 = iota((LEAF_DEV, 16), 1)
        acc = jnp.zeros((LEAF_DEV, NODES), F32)
        for c in range(8):
            hot = jnp.where((pcol == lane16) & (ccol == c), 1.0, 0.0).astype(BF16)
            acc = acc + dot(dot(hot, local_exp).astype(BF16), child_ops[c])
        leaf_local = acc.astype(BF16)
        fields = []
        for group in range(2):
            rows = leaf_local[group * 16 : group * 16 + 16]
            acc = jnp.zeros((16, PTS), F32)
            for r in range(0, 16, 2):
                both = jnp.concatenate([anterp[group * 16 + r], anterp[group * 16 + r + 1]], axis=1)
                pair = dot(rows, both)
                acc = jnp.where(row16 == r, pair[:, :PTS], jnp.where(row16 == r + 1, pair[:, PTS:], acc))
            fields.append(acc)
        return jnp.concatenate(fields, axis=0)

    own = pl.ds(HALO, LEAF_DEV)
    first, last = pl.ds(0, HALO), pl.ds(HALO, HALO)
    after = pl.ds(HALO + LEAF_DEV, HALO)
    q_pad[0, HALO : HALO + LEAF_DEV, :] = density[...]
    for load in loads[3:8]:
        load.wait()
    feat[24 * PAD :, :] = jnp.zeros((8 * PAD, PTS), F32)
    build_mask()
    for load in loads[8:]:
        load.wait()
    partial(0, density[...])
    pl.semaphore_wait(barrier, len(peers))
    sent = send_partial(0)
    halo = [
        remote(points.at[:, first], pts_pad.at[:, after], pt_ss.at[0], pt_rs.at[0], prev_dev),
        remote(points.at[:, last], pts_pad.at[:, first], pt_ss.at[1], pt_rs.at[1], next_dev),
    ]
    for copy in halo:
        copy.start()
    halo = halo + send_q(0, density)
    lists = [
        remote(far_list, fl_next, li_ss.at[0], li_rs.at[0], prev_dev),
        remote(far_list, fl_prev, li_ss.at[1], li_rs.at[1], next_dev),
        remote(far_op, fo_next, li_ss.at[2], li_rs.at[2], prev_dev),
        remote(far_op, fo_prev, li_ss.at[3], li_rs.at[3], next_dev),
    ]
    for copy in lists:
        copy.start()
    sent = sent + halo + lists
    for c in range(3):
        pts_pad[c, HALO : HALO + LEAF_DEV, :] = points[c]
    build_target(HALO, HALO + LEAF_DEV)
    own_multipole(0)
    copies = send_z(0)
    sent = sent + copies
    arrive(halo)
    build_target(0, HALO)
    build_source()
    build_halo()
    build_q(0)
    near_first(K_SPLIT[0], K_SPLIT[1])
    arrive(copies)
    sent = sent + gather_start(0)
    near_first(K_SPLIT[1], K_SPLIT[2])
    sent = sent + gather_middle(0)
    arrive(lists)
    build_codes()
    build_counts()
    near_first(K_SPLIT[2], K_SPLIT[3])
    sent = sent + gather_end(0)
    near_first(K_SPLIT[3], K_SPLIT[4])
    load_trans.wait()
    potential = FAR_WEIGHT * far_field(0) + NEAR_WEIGHT * near[...]
    q = density[...]
    q = q + DAMPING * (jnp.tanh(source[...] - potential) - q)

    q_pad[1, HALO : HALO + LEAF_DEV, :] = q
    halo = send_q(1, q_pad.at[1, own])
    partial(1, q)
    sent = sent + halo + send_partial(1)
    arrive(halo)
    build_q(1)
    own_multipole(1)
    copies = send_z(1)
    sent = sent + copies
    near_again(0, PAIRS // 2)
    arrive(copies)
    sent = sent + gather_start(1)
    near_again(PAIRS // 2, PAIRS)
    sent = sent + gather_middle(1)
    sent = sent + gather_end(1)
    potential = FAR_WEIGHT * far_field(1) + NEAR_WEIGHT * near[...]
    q = q_pad[1, HALO : HALO + LEAF_DEV, :]
    result[0] = q + DAMPING * (jnp.tanh(source[...] - potential) - q)
    result[1] = potential
    left(sent)


def solution(mesh):
    sizes = (mesh.shape["gx"], mesh.shape["gy"], mesh.shape["gz"])
    n_gx, n_gy, n_gz = sizes
    n_side = n_gy
    cols = 4 * n_gx * n_gy * n_gz
    vmem = pl.BlockSpec(memory_space=pltpu.VMEM)
    dma = pltpu.SemaphoreType.DMA

    def shards(points, *args):
        out = pl.pallas_call(
            functools.partial(kernel, sizes),
            out_shape=jax.ShapeDtypeStruct((2, LEAF_DEV, PTS), F32),
            in_specs=[pl.BlockSpec(memory_space=pl.ANY)] * 11,
            out_specs=vmem,
            scratch_shapes=[
                pltpu.VMEM((3, PAD, PTS), F32),
                pltpu.VMEM((2, PAD, PTS), F32),
                pltpu.VMEM((OCT_DEV, INTER), jnp.int32),
                pltpu.VMEM((OCT_DEV, INTER), jnp.int32),
                pltpu.VMEM((OCT_DEV, INTER), jnp.int32),
                pltpu.VMEM((OCT_DEV, INTER), jnp.int32),
                pltpu.VMEM((2, 4, 8, PTS), F32),
                pltpu.VMEM((2, 3, 8, PTS), F32),
                pltpu.VMEM((2, 2, n_side * n_side, n_gx, 8, PTS), BF16),
                pltpu.VMEM((PAD * PTS, 32), BF16),
                pltpu.VMEM((32, (HALO + LEAF_DEV) * PTS), BF16),
                pltpu.VMEM((32 * PAD, PTS), F32),
                pltpu.VMEM((8 * PAIRS, SPAN), F32),
                pltpu.VMEM((8, PAD * PTS), F32),
                pltpu.VMEM((PAIRS + SIDE, UPPER, 256), BF16),
                pltpu.VMEM((16, INTER), jnp.int32),
                pltpu.VMEM((16, INTER), jnp.int32),
                pltpu.VMEM((12 * OPS, cols), BF16),
                pltpu.VMEM((32 * OPS, PTS), F32),
                pltpu.VMEM((LEAF_DEV, PTS), F32),
                pltpu.VMEM((OPS, NODES, NODES), BF16),
                pltpu.VMEM((cols, INTER), jnp.int16),
                pltpu.VMEM((3, LEAF_DEV, PTS), F32),
                pltpu.VMEM((LEAF_DEV, PTS), F32),
                pltpu.VMEM((LEAF_DEV, PTS), F32),
                pltpu.VMEM((LEAF_DEV, NODES, PTS), BF16),
                pltpu.VMEM((LEAF_DEV,), jnp.int32),
                pltpu.VMEM((8, NODES, NODES), BF16),
                pltpu.VMEM((LEAF_DEV,), jnp.int32),
                pltpu.VMEM((LEAF_DEV, NEAR), jnp.int32),
                pltpu.VMEM((OCT_DEV, INTER), jnp.int32),
                pltpu.VMEM((OCT_DEV, INTER), jnp.int32),
                dma((10,)), dma, dma((2,)), dma((2,)), dma((2, 2)), dma((2, 2)), dma((4,)), dma((4,)), dma((2, 3)), dma((2, 3)),
                dma((2, n_gx - 1)), dma((2, n_gx - 1)),
                dma((2, n_side, n_side)), dma((2, n_side, n_side)), dma((2, n_side, n_side)), dma((2, n_side, n_side)),
            ],
            compiler_params=pltpu.CompilerParams(
                collective_id=0, has_side_effects=True, vmem_limit_bytes=60 * 1024 * 1024
            ),
        )(jnp.transpose(points, (1, 0, 2)), *args)
        return out[0], out[1]

    whole = ("gx", "gy", "gz")
    in_specs = (
        P(whole, None, None),
        P(whole, None),
        P(whole, None),
        P(whole, None, None),
        P(whole),
        P(),
        P(whole),
        P(whole, None),
        P(whole, None),
        P(whole, None),
        P(),
    )
    out_specs = (P(whole, None), P(whole, None))
    return jax.shard_map(shards, mesh=mesh, in_specs=in_specs, out_specs=out_specs, check_vma=False)
```

```python
import functools

import jax
import jax.numpy as jnp
from jax import lax
from jax.experimental import pallas as pl
from jax.experimental.pallas import tpu as pltpu
from jax.sharding import PartitionSpec as P

OPS = 16
ITERS = 2
SOFTEN = 0.01
DAMPING = 0.5
FAR_WEIGHT = 0.3
NEAR_WEIGHT = 0.03
PTS = 128
NODES = 216
INTER = 189
LEAF_DEV = 32
OCT_DEV = 4
NEAR = 27
HALO = 16
PAIRS = LEAF_DEV // 2
SIDE = 7
CHUNKS = 2 * SIDE + 1
SPAN = CHUNKS * 256
UPPER = SIDE * 256 + PTS
PAD = LEAF_DEV + 2 * HALO

MESH = pl.DeviceIdType.MESH
F32 = jnp.float32
BF16 = jnp.bfloat16
LAST = (((1,), (1,)), ((), ()))
K_SPLIT = (0, 0, 8, 14, 16)


def iota(shape, dim):
    return lax.broadcasted_iota(jnp.int32, shape, dim)


def dot(a, b):
    return jnp.dot(a, b, preferred_element_type=F32)


def dot_last(a, b):
    return lax.dot_general(a, b, LAST, preferred_element_type=F32)


def split3(v):
    first = v.astype(BF16).astype(F32)
    rest = v - first
    second = rest.astype(BF16).astype(F32)
    third = (rest - second).astype(BF16).astype(F32)
    return first, second, third


def kernel(
    sizes,
    points_hbm, source_hbm, density_hbm, anterp_hbm, child_slot_hbm, child_ops_hbm, parent_hbm, near_list_hbm, far_list_hbm, far_op_hbm, translations_hbm,
    result,
    pts_pad, q_pad, fl_prev, fl_next, fo_prev, fo_next, part_out, part_in, table,
    src_feat, tgt_feat, feat, mask_wide, q_wide, kmat, codes, ops, counts, grouped, near, trans, rows_of,
    points, source, density, anterp, child_slot, child_ops, parent, near_list, far_list, far_op,
    load_sem, tr_sem, pt_ss, pt_rs, q_ss, q_rs, li_ss, li_rs, pa_ss, pa_rs, z_ss, z_rs, a_ss, a_rs, c_ss, c_rs,
):
    n_gx, n_gy, n_gz = sizes
    n_x = n_gz // 2
    gx, gy, gz = lax.axis_index("gx"), lax.axis_index("gy"), lax.axis_index("gz")
    device = (gx * n_gy + gy) * n_gz + gz
    xx, core = gz // 2, gz % 2
    prev_gz, next_gz = (gz + n_gz - 1) % n_gz, (gz + 1) % n_gz
    fast = gy + core * (xx - gy)
    slow = xx + core * (gy - xx)
    n_side = n_gy

    def z_peer(s):
        return ((gx + s) % n_gx, gy, gz)

    offsets = [(i, j) for i in range(n_side) for j in range(n_side) if i or j]
    offsets.sort(key=lambda o: min(o[0], n_side - o[0]) + min(o[1], n_side - o[1]))

    def side_peer(i, j):
        a, b = (slow + i) % n_side, (fast + j) % n_side
        return (gx, b + core * (a - b), 2 * (a + core * (b - a)) + core)

    sibling = (gx, gy, gz + 1 - 2 * core)
    prev_dev, next_dev = (gx, gy, prev_gz), (gx, gy, next_gz)
    outer = (gx, gy, prev_gz + core * (next_gz - prev_gz))
    outer_x = (xx + n_x - 1 + 2 * core) % n_x

    def spot(a, b):
        return (a + core * (b - a)) * n_side + b + core * (a - b)

    def piece(it, i, j):
        return table.at[it, core, spot((slow + i) % n_side, (fast + j) % n_side)]

    barrier = pltpu.get_barrier_semaphore()
    peers = [z_peer(s) for s in range(1, n_gx)] + [side_peer(i, j) for i, j in offsets] + [sibling, outer]
    for peer in peers:
        pl.semaphore_signal(barrier, inc=1, device_id=peer, device_id_type=MESH)

    loads = [
        pltpu.make_async_copy(src, dst, load_sem.at[k])
        for k, (src, dst) in enumerate(
            (
                (density_hbm, density), (parent_hbm, parent), (child_slot_hbm, child_slot), (near_list_hbm, near_list),
                (points_hbm, points), (far_list_hbm, far_list), (far_op_hbm, far_op), (source_hbm, source),
                (anterp_hbm, anterp), (child_ops_hbm, child_ops),
            )
        )
    ]
    for load in loads:
        load.start()
    load_trans = pltpu.make_async_copy(translations_hbm, trans, tr_sem)
    load_trans.start()
    for load in loads[:3]:
        load.wait()
    pslot = parent[...].reshape(1, LEAF_DEV) - (device * OCT_DEV - OCT_DEV)
    cslot = child_slot[...].reshape(1, LEAF_DEV)
    square = iota((LEAF_DEV, LEAF_DEV), 0) == iota((LEAF_DEV, LEAF_DEV), 1)
    pcol = jnp.sum(jnp.where(square, pslot.astype(F32), 0.0), axis=1, keepdims=True).astype(jnp.int32)
    ccol = jnp.sum(jnp.where(square, cslot.astype(F32), 0.0), axis=1, keepdims=True).astype(jnp.int32)
    chip_slot = parent[...].reshape(1, LEAF_DEV) - (device - core) * OCT_DEV
    part_row = iota((16, LEAF_DEV), 0)
    part_row = jnp.where(part_row < 8, part_row, part_row - 16 + 16 * core)
    row16 = iota((16, 1), 0)

    def remote(src, dst, ss, rs, dev):
        return pltpu.make_async_remote_copy(
            src_ref=src, dst_ref=dst, send_sem=ss, recv_sem=rs, device_id=dev, device_id_type=MESH
        )

    def partial(it, q32):
        q_b = q32.astype(BF16).astype(F32)
        mult = []
        for group in range(2):
            rows = q_b[group * 16 : group * 16 + 16]
            acc = jnp.zeros((16, NODES), F32)
            for r in range(0, 16, 2):
                lhs = jnp.concatenate([jnp.where(row16 == r + k, rows, 0.0) for k in range(2)], axis=1).astype(BF16)
                both = jnp.concatenate([anterp[group * 16 + r], anterp[group * 16 + r + 1]], axis=1)
                acc = acc + dot_last(lhs, both)
            mult.append(acc)
        leaf_mult = jnp.concatenate(mult, axis=0).astype(BF16)
        acc = jnp.zeros((16, NODES), F32)
        for c in range(8):
            hot = jnp.where((part_row == chip_slot) & (cslot == c), 1.0, 0.0).astype(BF16)
            acc = acc + dot_last(dot(hot, leaf_mult).astype(BF16), child_ops[c])
        low = acc[:, :PTS]
        high = jnp.concatenate([acc[:, PTS:], jnp.zeros((16, 256 - NODES), F32)], axis=1)
        part_out[it, 0] = jnp.where(core == 0, high[:8], low[:8])
        part_out[it, 1] = low[8:]
        part_out[it, 2] = high[8:]
        part_out[it, 3] = jnp.where(core == 0, low[:8], high[:8])

    def send_partial(it):
        copies = [remote(part_out.at[it, 0], part_in.at[it, 0], pa_ss.at[it, 0], pa_rs.at[it, 0], sibling)]
        for h in range(2):
            copies.append(
                remote(
                    part_out.at[it, 1 + h], part_in.at[it, 2 - core], pa_ss.at[it, 1 + h], pa_rs.at[it, 2 - core],
                    (gx, gy, 2 * outer_x + h),
                )
            )
        for copy in copies:
            copy.start()
        return copies

    def own_multipole(it):
        for k in range(3):
            remote(part_out.at[it, k], part_in.at[it, k], pa_ss.at[it, k], pa_rs.at[it, k], sibling).wait_recv()
        total = part_out[it, 3] + part_in[it, 0] + part_in[it, 1] + part_in[it, 2]
        table[it, core, spot(slow, fast), gx] = total.astype(BF16)

    def send_q(it, src):
        copies = [
            remote(src.at[pl.ds(0, HALO)], q_pad.at[it, pl.ds(HALO + LEAF_DEV, HALO)], q_ss.at[it, 0], q_rs.at[it, 0], prev_dev),
            remote(src.at[pl.ds(HALO, HALO)], q_pad.at[it, pl.ds(0, HALO)], q_ss.at[it, 1], q_rs.at[it, 1], next_dev),
        ]
        for copy in copies:
            copy.start()
        return copies

    def send_z(it):
        block = table.at[it, core, spot(slow, fast), pl.ds(gx, 1)]
        copies = [remote(block, block, z_ss.at[it, s - 1], z_rs.at[it, s - 1], z_peer(s)) for s in range(1, n_gx)]
        for copy in copies:
            copy.start()
        return copies

    def side_copy(it, i, j):
        block = piece(it, 0, 0)
        return remote(block, block, a_ss.at[it, i, j], a_rs.at[it, i, j], side_peer(i, j))

    def core_copy(it, i, j):
        block = piece(it, i, j)
        return remote(block, block, c_ss.at[it, i, j], c_rs.at[it, i, j], sibling)

    def gather_start(it):
        copies = [side_copy(it, i, j) for i, j in offsets[::-1]] + [core_copy(it, 0, 0)]
        for copy in copies:
            copy.start()
        return copies

    def forward(it, batch):
        sent = []
        for i, j in batch:
            side_copy(it, i, j).wait_recv()
            copy = core_copy(it, (n_side - i) % n_side, (n_side - j) % n_side)
            copy.start()
            sent.append(copy)
        return sent

    def gather_middle(it):
        return forward(it, offsets[: len(offsets) // 2])

    def gather_end(it):
        return forward(it, offsets[len(offsets) // 2 :])

    def gather_wait(it):
        for i in range(n_side):
            for j in range(n_side):
                core_copy(it, i, j).wait_recv()

    def arrive(copies):
        for copy in copies:
            copy.wait_recv()

    def left(copies):
        for copy in copies:
            copy.wait_send()

    def planes(lo, hi, values):
        for f, value in enumerate(values):
            feat[f * PAD + lo : f * PAD + hi, :] = value

    def build_source():
        parts = [split3(pts_pad[c]) for c in range(3)]
        norm = split3(pts_pad[0] * pts_pad[0] + pts_pad[1] * pts_pad[1] + pts_pad[2] * pts_pad[2])
        values = [parts[c][k] for k in (0, 0, 1, 1, 0, 2) for c in range(3)] + list(norm) + [jnp.ones((PAD, PTS), F32)] * 3
        planes(0, PAD, values)

        def body(w, carry):
            tile = jnp.transpose(feat[pl.ds(w, 32, stride=PAD), :]).astype(BF16)
            src_feat[pl.ds(pl.multiple_of(w * PTS, PTS), PTS), :] = tile
            return carry

        lax.fori_loop(2, PAD - 2, body, 0, unroll=4)

    def build_target(lo, hi):
        pts = [pts_pad[c, lo:hi] for c in range(3)]
        parts = [[-2.0 * v for v in split3(p)] for p in pts]
        norm = split3(pts[0] * pts[0] + pts[1] * pts[1] + pts[2] * pts[2] + SOFTEN)
        values = [parts[c][k] for k in (0, 1, 0, 1, 2, 0) for c in range(3)]
        planes(lo, hi, values + [jnp.ones((hi - lo, PTS), F32)] * 3 + list(norm))

        def body(w, carry):
            tgt_feat[:, pl.ds(pl.multiple_of(w * PTS, PTS), PTS)] = feat[pl.ds(w, 32, stride=PAD), :].astype(BF16)
            return carry

        lax.fori_loop(lo, hi, body, 0, unroll=8)

    def build_mask():
        listed = near_list[...]
        leaf = iota((LEAF_DEV, 1), 0)
        first = device * LEAF_DEV - 2 * SIDE + 2 * (leaf // 2)
        slot = jnp.where(listed >= 0, listed - first, -1)
        lane = iota((LEAF_DEV, PTS), 1)
        mask = jnp.zeros((LEAF_DEV, PTS), F32)
        for k in range(NEAR):
            mask = jnp.where(slot[:, k : k + 1] == lane, 1.0, mask)
        r = iota((8 * PAIRS, LEAF_DEV), 0)
        pick = (r // 8 * 2 + (r % 8) // 2 == iota((8 * PAIRS, LEAF_DEV), 1)) & (r % 8 < 4)
        rows = dot(jnp.where(pick, 1.0, 0.0).astype(BF16), mask.astype(BF16)).astype(BF16)
        for c in range(CHUNKS):
            spread = iota((PTS, 256), 0) == 2 * c + iota((PTS, 256), 1) // PTS
            mask_wide[:, c * 256 : c * 256 + 256] = dot(rows, jnp.where(spread, 1.0, 0.0).astype(BF16))

    def build_q(it):
        even = iota((8, PTS), 0) % 2 == 0
        for w in range(PAD):
            row = q_pad[it, w : w + 1, :]
            high = row.astype(BF16).astype(F32)
            q_wide[:, w * PTS : w * PTS + PTS] = jnp.where(even, high, row - high)

    def store_near(t, acc):
        near[pl.ds(2 * t, 1), :] = acc[0:1, :PTS] + acc[1:2, :PTS]
        near[pl.ds(2 * t + 1, 1), :] = acc[2:3, PTS:] + acc[3:4, PTS:]

    def near_lhs(t, c):
        start = pl.multiple_of((t + HALO // 2 - SIDE + c) * 256, 256)
        rows = pl.ds(pl.multiple_of(8 * t, 8), 8)
        return (mask_wide[rows, c * 256 : c * 256 + 256] * q_wide[:, pl.ds(start, 256)]).astype(BF16)

    def build_halo():
        for e in range(SIDE):
            target = tgt_feat[:, (e + 1) * 256 : (e + 2) * 256]
            tile = dot(src_feat[HALO * PTS : HALO * PTS + (e + 1) * 256 - PTS, :], target)
            kmat[e, (SIDE - e) * 256 :, :] = lax.rsqrt(tile.astype(BF16))

    def near_again(t0, t1):
        def body(t, carry):
            acc = jnp.zeros((8, 256), F32)
            for o in range(SIDE):
                acc = acc + dot(near_lhs(t, SIDE + o), kmat[t + SIDE, o * 256 : o * 256 + 256, :])
            acc = acc + dot(near_lhs(t, 2 * SIDE)[:, :PTS], kmat[t + SIDE, SIDE * 256 :, :])
            for o in range(1, SIDE):
                acc = acc + dot_last(near_lhs(t, SIDE - o), kmat[t + SIDE - o, o * 256 : o * 256 + 256, :])
            edge = dot_last(near_lhs(t, 0), kmat[t, SIDE * 256 :, :])
            acc = acc + jnp.concatenate([edge, jnp.zeros((8, PTS), F32)], axis=1)
            store_near(t, acc)
            return carry

        lax.fori_loop(t0, t1, body, 0, unroll=2)

    def near_first(t0, t1):
        def body(t, carry):
            start = pl.multiple_of((t + HALO // 2) * 256, 256)
            target = tgt_feat[:, pl.ds(start, 256)]
            kmat[t + SIDE] = lax.rsqrt(dot(src_feat[pl.ds(start, UPPER), :], target).astype(BF16))
            return carry

        lax.fori_loop(t0, t1, body, 0, unroll=2)
        near_again(t0, t1)

    def build_codes():
        lg = n_gz.bit_length() - 1
        ly = n_gy.bit_length() - 1
        for row, lists, kinds in ((0, fl_prev, fo_prev), (4, far_list, far_op), (8, fl_next, fo_next)):
            s = lists[...]
            d = s >> 2
            sx = (d & (n_gz - 1)) >> 1
            sy = (d >> lg) & (n_gy - 1)
            sg = d >> (lg + ly)
            codes[row : row + 4, :] = ((sx * n_gy + sy) * n_gx + sg) * 8 + (s & 7)
            ops[row : row + 4, :] = kinds[...]

    def build_counts():
        cols = 8 * n_side * n_side * n_gx
        width = min(256, cols)
        rows_of[...] = iota((cols, INTER), 0).astype(jnp.int16)
        for start in (12 * OPS, 28 * OPS):
            grouped[start : start + 4 * OPS, :] = jnp.zeros((4 * OPS, PTS), F32)

        def body(g, carry):
            code16 = jnp.broadcast_to(codes[pl.ds(g, 1), :], (16, INTER)).astype(jnp.int16)
            code16 = jnp.broadcast_to(code16[:1], (width, INTER))
            one16, zero16 = jnp.ones((width, INTER), BF16), jnp.zeros((width, INTER), BF16)
            kind = jnp.where(iota((OPS, INTER), 0) == ops[pl.ds(g, 1), :], 1.0, 0.0).astype(BF16)
            rows = pl.ds(pl.multiple_of(g * OPS, OPS), OPS)
            for c in range(cols // width):
                hot = jnp.where(rows_of[c * width : (c + 1) * width, :] == code16, one16, zero16)
                counts[rows, c * width : (c + 1) * width] = dot_last(kind, hot).astype(BF16)
            return carry

        lax.fori_loop(0, 12, body, 0)
    def far_field(it):
        gather_wait(it)
        cols = 8 * n_side * n_side * n_gx
        blocks = jnp.concatenate([table[it, 0].reshape(cols, PTS), table[it, 1].reshape(cols, PTS)], axis=1)
        both = dot(counts[...], blocks)
        grouped[0 : 12 * OPS, :] = both[:, :PTS]
        grouped[16 * OPS : 28 * OPS, :] = both[:, PTS:]
        acc = jnp.zeros((32, NODES), F32)
        for o in range(OPS):
            full = jnp.concatenate(
                [grouped[pl.ds(o, 16, stride=16), :], grouped[pl.ds(256 + o, 16, stride=16), :]], axis=1
            )[:, :NODES]
            high = full.astype(BF16)
            low = (full - high.astype(F32)).astype(BF16)
            acc = acc + dot_last(jnp.concatenate([high, low], axis=0), trans[o])
        local_exp = (acc[:16] + acc[16:]).astype(BF16)
        lane16 = iota((LEAF_DEV, 16), 1)
        acc = jnp.zeros((LEAF_DEV, NODES), F32)
        for c in range(8):
            hot = jnp.where((pcol == lane16) & (ccol == c), 1.0, 0.0).astype(BF16)
            acc = acc + dot(dot(hot, local_exp).astype(BF16), child_ops[c])
        leaf_local = acc.astype(BF16)
        fields = []
        for group in range(2):
            rows = leaf_local[group * 16 : group * 16 + 16]
            acc = jnp.zeros((16, PTS), F32)
            for r in range(0, 16, 2):
                both = jnp.concatenate([anterp[group * 16 + r], anterp[group * 16 + r + 1]], axis=1)
                pair = dot(rows, both)
                acc = jnp.where(row16 == r, pair[:, :PTS], jnp.where(row16 == r + 1, pair[:, PTS:], acc))
            fields.append(acc)
        return jnp.concatenate(fields, axis=0)

    own = pl.ds(HALO, LEAF_DEV)
    first, last = pl.ds(0, HALO), pl.ds(HALO, HALO)
    after = pl.ds(HALO + LEAF_DEV, HALO)
    q_pad[0, HALO : HALO + LEAF_DEV, :] = density[...]
    for load in loads[3:8]:
        load.wait()
    feat[24 * PAD :, :] = jnp.zeros((8 * PAD, PTS), F32)
    build_mask()
    for load in loads[8:]:
        load.wait()
    partial(0, density[...])
    pl.semaphore_wait(barrier, len(peers))
    sent = send_partial(0)
    halo = [
        remote(points.at[:, first], pts_pad.at[:, after], pt_ss.at[0], pt_rs.at[0], prev_dev),
        remote(points.at[:, last], pts_pad.at[:, first], pt_ss.at[1], pt_rs.at[1], next_dev),
    ]
    for copy in halo:
        copy.start()
    halo = halo + send_q(0, density)
    lists = [
        remote(far_list, fl_next, li_ss.at[0], li_rs.at[0], prev_dev),
        remote(far_list, fl_prev, li_ss.at[1], li_rs.at[1], next_dev),
        remote(far_op, fo_next, li_ss.at[2], li_rs.at[2], prev_dev),
        remote(far_op, fo_prev, li_ss.at[3], li_rs.at[3], next_dev),
    ]
    for copy in lists:
        copy.start()
    sent = sent + halo + lists
    for c in range(3):
        pts_pad[c, HALO : HALO + LEAF_DEV, :] = points[c]
    build_target(HALO, HALO + LEAF_DEV)
    own_multipole(0)
    copies = send_z(0)
    sent = sent + copies
    arrive(halo)
    build_target(0, HALO)
    build_source()
    build_halo()
    build_q(0)
    near_first(K_SPLIT[0], K_SPLIT[1])
    arrive(copies)
    sent = sent + gather_start(0)
    near_first(K_SPLIT[1], K_SPLIT[2])
    sent = sent + gather_middle(0)
    arrive(lists)
    build_codes()
    build_counts()
    near_first(K_SPLIT[2], K_SPLIT[3])
    sent = sent + gather_end(0)
    near_first(K_SPLIT[3], K_SPLIT[4])
    load_trans.wait()
    potential = FAR_WEIGHT * far_field(0) + NEAR_WEIGHT * near[...]
    q = density[...]
    q = q + DAMPING * (jnp.tanh(source[...] - potential) - q)

    q_pad[1, HALO : HALO + LEAF_DEV, :] = q
    halo = send_q(1, q_pad.at[1, own])
    partial(1, q)
    earlier = sent
    sent = halo + send_partial(1)
    arrive(halo)
    build_q(1)
    own_multipole(1)
    copies = send_z(1)
    sent = sent + copies
    near_again(0, PAIRS // 2)
    arrive(copies)
    sent = sent + gather_start(1)
    near_again(PAIRS // 2, PAIRS)
    left(earlier)
    sent = sent + gather_middle(1)
    sent = sent + gather_end(1)
    potential = FAR_WEIGHT * far_field(1) + NEAR_WEIGHT * near[...]
    q = q_pad[1, HALO : HALO + LEAF_DEV, :]
    result[0] = q + DAMPING * (jnp.tanh(source[...] - potential) - q)
    result[1] = potential
    left(sent)


def solution(mesh):
    sizes = (mesh.shape["gx"], mesh.shape["gy"], mesh.shape["gz"])
    n_gx, n_gy, n_gz = sizes
    n_side = n_gy
    cols = 4 * n_gx * n_gy * n_gz
    vmem = pl.BlockSpec(memory_space=pltpu.VMEM)
    dma = pltpu.SemaphoreType.DMA

    def shards(points, *args):
        out = pl.pallas_call(
            functools.partial(kernel, sizes),
            out_shape=jax.ShapeDtypeStruct((2, LEAF_DEV, PTS), F32),
            in_specs=[pl.BlockSpec(memory_space=pl.ANY)] * 11,
            out_specs=vmem,
            scratch_shapes=[
                pltpu.VMEM((3, PAD, PTS), F32),
                pltpu.VMEM((2, PAD, PTS), F32),
                pltpu.VMEM((OCT_DEV, INTER), jnp.int32),
                pltpu.VMEM((OCT_DEV, INTER), jnp.int32),
                pltpu.VMEM((OCT_DEV, INTER), jnp.int32),
                pltpu.VMEM((OCT_DEV, INTER), jnp.int32),
                pltpu.VMEM((2, 4, 8, PTS), F32),
                pltpu.VMEM((2, 3, 8, PTS), F32),
                pltpu.VMEM((2, 2, n_side * n_side, n_gx, 8, PTS), BF16),
                pltpu.VMEM((PAD * PTS, 32), BF16),
                pltpu.VMEM((32, (HALO + LEAF_DEV) * PTS), BF16),
                pltpu.VMEM((32 * PAD, PTS), F32),
                pltpu.VMEM((8 * PAIRS, SPAN), F32),
                pltpu.VMEM((8, PAD * PTS), F32),
                pltpu.VMEM((PAIRS + SIDE, UPPER, 256), BF16),
                pltpu.VMEM((16, INTER), jnp.int32),
                pltpu.VMEM((16, INTER), jnp.int32),
                pltpu.VMEM((12 * OPS, cols), BF16),
                pltpu.VMEM((32 * OPS, PTS), F32),
                pltpu.VMEM((LEAF_DEV, PTS), F32),
                pltpu.VMEM((OPS, NODES, NODES), BF16),
                pltpu.VMEM((cols, INTER), jnp.int16),
                pltpu.VMEM((3, LEAF_DEV, PTS), F32),
                pltpu.VMEM((LEAF_DEV, PTS), F32),
                pltpu.VMEM((LEAF_DEV, PTS), F32),
                pltpu.VMEM((LEAF_DEV, NODES, PTS), BF16),
                pltpu.VMEM((LEAF_DEV,), jnp.int32),
                pltpu.VMEM((8, NODES, NODES), BF16),
                pltpu.VMEM((LEAF_DEV,), jnp.int32),
                pltpu.VMEM((LEAF_DEV, NEAR), jnp.int32),
                pltpu.VMEM((OCT_DEV, INTER), jnp.int32),
                pltpu.VMEM((OCT_DEV, INTER), jnp.int32),
                dma((10,)), dma, dma((2,)), dma((2,)), dma((2, 2)), dma((2, 2)), dma((4,)), dma((4,)), dma((2, 3)), dma((2, 3)),
                dma((2, n_gx - 1)), dma((2, n_gx - 1)),
                dma((2, n_side, n_side)), dma((2, n_side, n_side)), dma((2, n_side, n_side)), dma((2, n_side, n_side)),
            ],
            compiler_params=pltpu.CompilerParams(
                collective_id=0, has_side_effects=True, vmem_limit_bytes=60 * 1024 * 1024
            ),
        )(jnp.transpose(points, (1, 0, 2)), *args)
        return out[0], out[1]

    whole = ("gx", "gy", "gz")
    in_specs = (
        P(whole, None, None),
        P(whole, None),
        P(whole, None),
        P(whole, None, None),
        P(whole),
        P(),
        P(whole),
        P(whole, None),
        P(whole, None),
        P(whole, None),
        P(),
    )
    out_specs = (P(whole, None), P(whole, None))
    return jax.shard_map(shards, mesh=mesh, in_specs=in_specs, out_specs=out_specs, check_vma=False)
```
